32 devices in a mesh: dp: 8 (over z, x), mp: 4 (over y, core).
Axes of the slice: x: 2, y: 2, z: 4, core: 2. Of those that a mesh axis runs over, the one named last changes fastest.
Arguments:
- hidden_in: bfloat16 [8192, 1024], P(('dp', 'mp')), may hold values from -6 to 6
- doc_index: int32 [8192], P('dp'), may hold values from 0 to 256, as said below
- doc_position: int32 [8192], P('dp'), may hold values from 0 to 767, as said below
- w_query: bfloat16 [1024, 1024], P(None, 'mp'), may hold values from -0.1875 to 0.1875
- w_key: bfloat16 [1024, 1024], P(None, 'mp'), may hold values from -0.1875 to 0.1875
- w_value: bfloat16 [1024, 1024], P(None, 'mp'), may hold values from -0.1875 to 0.1875
- w_out: bfloat16 [1024, 1024], P('mp'), may hold values from -0.1875 to 0.1875
- w_up: bfloat16 [1024, 4096], P(None, 'mp'), may hold values from -0.1875 to 0.1875
- w_gate: bfloat16 [1024, 4096], P(None, 'mp'), may hold values from -0.1875 to 0.1875
- w_down: bfloat16 [4096, 1024], P('mp'), may hold values from -0.09375 to 0.09375
- score_scale: float32 [1024], P('mp'), may hold values from 1 to 1.7
- up_scale: float32 [4096], P('mp'), may hold values from 0.5 to 2
- gate_scale: float32 [4096], P('mp'), may hold values from 0.5 to 2
- alpha_attention: float32 [1024], replicated, may hold values from 0.2 to 0.6
- alpha_feedforward: float32 [1024], replicated, may hold values from 0.2 to 0.6
- cotangent: bfloat16 [8192, 1024], P(('dp', 'mp'))
Outputs:
- layer_out: bfloat16 [8192, 1024], P(('dp', 'mp'))
- grad_input: float32 [8192, 1024], P(('dp', 'mp'))
- grad_query: float32 [1024, 1024], P('dp', 'mp')
- grad_key: float32 [1024, 1024], P('dp', 'mp')
- grad_value: float32 [1024, 1024], P('dp', 'mp')
- grad_out: float32 [1024, 1024], P('mp', 'dp')
- grad_up: float32 [1024, 4096], P('dp', 'mp')
- grad_gate: float32 [1024, 4096], P('dp', 'mp')
- grad_down: float32 [4096, 1024], P('mp', 'dp')
- grad_score_scale: float32 [1024], P(('mp', 'dp'))
- grad_up_scale: float32 [4096], P(('mp', 'dp'))
- grad_gate_scale: float32 [4096], P(('mp', 'dp'))
- grad_alpha_attention: float32 [1024], P(('mp', 'dp'))
- grad_alpha_feedforward: float32 [1024], P(('mp', 'dp'))
The draws below stay inside these ranges and needn't reach their ends.
Inputs may be any that keep to these rules, and one draw needn't show every extreme that they name: `doc_index`: within each sequence of 1024 tokens, document numbers start at 0 on its first token and rise by one at each document start; one document of exactly 768 tokens begins within the sequence's first 256 tokens and ends within its last 256. `doc_position`: counts tokens from 0 at the first token of each document.
All inputs are finite; a program needn't handle non-finite values.
Results may differ from the reference program's by a relative error of at most 0.025.
Values may be sent and summed in bfloat16 or wider, within the bound.
No kernel may reach another device: no remote copies, remote signals or barrier semaphores. Data moves between devices by JAX's collectives and lax.ppermute only.
A program may use at most 128 MiB of HBM per device.

```python
import math
import jax
import jax.numpy as jnp
from jax import lax

D = 1024
HEADS = 16
HEAD_DIM = 64
FF = 4096
TOK_DEV = 256
SEQ = 1024
TOKENS = 8192
N_DP = 8
N_MP = 4


def doc_layout(key):
    seq_len = TOK_DEV * N_MP
    first_long = jax.random.randint(jax.random.fold_in(key, 11), (N_DP, 1), 1, TOK_DEV)
    last_long = first_long + (seq_len - TOK_DEV)
    token_index = jnp.arange(seq_len).astype(jnp.int32)[None, :]
    seq_number = jnp.arange(N_DP).astype(jnp.int32)[:, None]
    cut_draw = jax.random.randint(jax.random.fold_in(key, 13), (N_DP, seq_len), 0, 24)
    outside = (token_index < first_long) | (token_index >= last_long)
    starts = ((cut_draw == 0) | (seq_number == 0)) & outside | (token_index == 0) | (token_index == first_long) | (token_index == last_long)
    doc_numbers = jnp.cumsum(starts.astype(jnp.int32), axis=1) - 1
    begins = lax.cummax(jnp.where(starts, token_index, 0), axis=1)
    return (doc_numbers.reshape(-1).astype(jnp.int32), (token_index - begins).reshape(-1).astype(jnp.int32))


def draw_doc_index(key, part):
    return doc_layout(key)[0]


def draw_doc_position(key, part):
    return doc_layout(key)[1]


def draw_cotangent(key, part):
    row_index = jnp.arange(TOKENS).astype(jnp.float32)[:, None]
    row_factor = jnp.exp(jnp.log(3.0) * row_index / max(TOKENS - 1, 1))
    values_drawn = jax.random.normal(key, (TOKENS, D), jnp.float32)
    return (values_drawn * row_factor).astype(jnp.bfloat16)


def level_of(stream_key, dims, cuts, smallest, high):
    factor_of, own = 1.0, jax.random.fold_in(stream_key, 6)
    for dim, blocks in cuts:
        heights = jnp.exp(jax.random.uniform(jax.random.fold_in(own, dim), (blocks,), jnp.float32, smallest / len(cuts), high / len(cuts)))
        factor_of = factor_of * jnp.repeat(heights, dims[dim] // blocks).reshape([-1 if axis == dim else 1 for axis in range(len(dims))])
    return factor_of


def normal_values(key, dims, deviation, most, cuts=(), kind=jnp.bfloat16):
    values = deviation * jax.random.normal(key, dims, jnp.float32)
    if cuts:
        values = values * level_of(key, dims, cuts, -0.22, 0.18)
    return jnp.clip(values, -most, most).astype(kind)


def setup_inputs(seed: int = 0) -> dict:
    keys = jax.random.split(jax.random.key(seed), 17)
    return {
        "hidden_in": normal_values(keys[0], (TOKENS, D), 1.0, 6.0, ((0, 32),)),
        "doc_index": draw_doc_index(jax.random.fold_in(keys[16], 71), 0),
        "doc_position": draw_doc_position(jax.random.fold_in(keys[16], 71), 0),
        "w_query": normal_values(keys[3], (D, D), D ** -0.5, 0.1875, ((1, 4),)),
        "w_key": normal_values(keys[4], (D, D), D ** -0.5, 0.1875, ((1, 4),)),
        "w_value": normal_values(keys[5], (D, D), D ** -0.5, 0.1875, ((1, 4),)),
        "w_out": normal_values(keys[6], (D, D), D ** -0.5, 0.1875, ((0, 4),)),
        "w_up": normal_values(keys[7], (D, FF), D ** -0.5, 0.1875, ((1, 4),)),
        "w_gate": normal_values(keys[8], (D, FF), D ** -0.5, 0.1875, ((1, 4),)),
        "w_down": normal_values(keys[9], (FF, D), FF ** -0.5, 0.09375, ((0, 4),)),
        "score_scale": jnp.clip(jnp.exp(math.log(1.7) - 0.53062828 * jax.random.uniform(keys[10], (D,), jnp.float32) ** level_of(keys[10], (D,), ((0, 4),), -0.2, 0.2)), 1.0, 1.7),
        "up_scale": jnp.clip(jnp.exp(math.log(2.0) - 1.3862944 * jax.random.uniform(keys[11], (FF,), jnp.float32) ** level_of(keys[11], (FF,), ((0, 4),), -0.2, 0.2)), 0.5, 2.0),
        "gate_scale": jnp.clip(jnp.exp(math.log(2.0) - 1.3862944 * jax.random.uniform(keys[12], (FF,), jnp.float32) ** level_of(keys[12], (FF,), ((0, 4),), -0.2, 0.2)), 0.5, 2.0),
        "alpha_attention": jnp.clip(jax.random.uniform(keys[13], (D,), jnp.float32, 0.2, 0.6), 0.2, 0.6),
        "alpha_feedforward": jnp.clip(jax.random.uniform(keys[14], (D,), jnp.float32, 0.2, 0.6), 0.2, 0.6),
        "cotangent": draw_cotangent(jax.random.fold_in(keys[16], 71), 0),
    }


@jax.custom_vjp
def low(v):
    return lax.optimization_barrier(v.astype(jnp.bfloat16)).astype(jnp.float32)

@jax.custom_vjp
def low_back(v):
    return v

def low_keep(v):
    return (low(v), None)

def low_pass(kept, grad):
    return (grad,)

def back_keep(v):
    return (v, None)

def back_low(kept, grad):
    return (low(grad),)
low.defvjp(low_keep, low_pass)
low_back.defvjp(back_keep, back_low)
epsilon = 1e-06
highest = lax.Precision.HIGHEST
masked_fill = -1e+30

def product(left, right):
    return jnp.dot(left, right, precision=highest, preferred_element_type=jnp.float32)

def sphere(values):
    return values * lax.rsqrt(lax.optimization_barrier(jnp.mean(values * values, axis=-1, keepdims=True)) + epsilon)

def rotate(values, positions):
    half_dim = values.shape[-1] // 2
    steps_half = jnp.arange(half_dim).astype(jnp.float32)
    inverse = jnp.exp(steps_half * (-2.0 * jnp.log(10000.0) / values.shape[-1]))
    angles = positions.astype(jnp.float32)[:, None] * inverse[None, :]
    cosine = jnp.cos(angles)[:, None, :]
    sine = jnp.sin(angles)[:, None, :]
    first_half = values[..., :half_dim]
    second_half = values[..., half_dim:]
    return jnp.concatenate([first_half * cosine - second_half * sine, second_half * cosine + first_half * sine], axis=-1)

def attend(queries, key_heads, value_heads, doc_rows):
    seq_len = queries.shape[1]
    block_rows = 512 if seq_len % 512 == 0 else seq_len
    scale_factor = 1.0 / queries.shape[2] ** 0.5
    col_index = jnp.arange(seq_len).astype(jnp.int32)

    def one_block(first_row):
        query_block = lax.dynamic_slice_in_dim(queries, first_row, block_rows, 1)
        row_index = first_row + jnp.arange(block_rows).astype(jnp.int32)
        row_docs = lax.dynamic_slice_in_dim(doc_rows, first_row, block_rows, 0)
        allowed = (row_docs[:, None] == doc_rows[None, :]) & (col_index[None, :] <= row_index[:, None])
        raw_scores = low_back(jnp.einsum('hqd,hkd->hqk', query_block, key_heads, precision=highest))
        scores = jnp.where(allowed[None], raw_scores * scale_factor, masked_fill)
        row_max = lax.optimization_barrier(jnp.max(scores, axis=-1, keepdims=True))
        exponent = jnp.exp(scores - row_max)
        probability = low(exponent / lax.optimization_barrier(jnp.sum(exponent, axis=-1, keepdims=True)))
        return jnp.einsum('hqk,hkd->hqd', probability, value_heads, precision=highest)
    firsts = (jnp.arange(seq_len // block_rows) * block_rows).astype(jnp.int32)
    blocks_out = lax.map(jax.checkpoint(one_block), firsts)
    return jnp.transpose(blocks_out, (1, 0, 2, 3)).reshape(queries.shape)

def block_forward(params, hidden, doc_rows, positions):
    w_query, w_key, w_value, w_out, w_up, w_gate, w_down, score_scale, up_scale, gate_scale, alpha_attention, alpha_feedforward = params
    seq_len = hidden.shape[0]
    query0 = low_back(product(hidden, w_query))
    key0 = low_back(product(hidden, w_key))
    value0 = low_back(product(hidden, w_value))
    head_shape = (seq_len, HEADS, HEAD_DIM)
    scales = score_scale.reshape(HEADS, HEAD_DIM)
    queries = low(sphere(rotate(query0.reshape(head_shape), positions)) * scales)
    key_heads = low(sphere(rotate(key0.reshape(head_shape), positions)) * scales)
    value_heads = low(value0.reshape(head_shape))
    attended = attend(queries.transpose(1, 0, 2), key_heads.transpose(1, 0, 2), value_heads.transpose(1, 0, 2), doc_rows)
    attended = low(low_back(attended.transpose(1, 0, 2).reshape(seq_len, D)))
    mixed_attn = low_back(product(attended, w_out))
    middle = sphere(hidden + alpha_attention * (sphere(mixed_attn) - hidden))
    middle_low = low(middle)
    up_part = low_back(product(middle_low, w_up)) * up_scale
    gate_part = low_back(product(middle_low, w_gate)) * gate_scale
    inner = low(up_part * jax.nn.silu(gate_part))
    mixed_ff = low_back(product(inner, w_down))
    return sphere(middle + alpha_feedforward * (sphere(mixed_ff) - middle))

def reference(hidden_in, doc_index, doc_position, w_query, w_key, w_value, w_out, w_up, w_gate, w_down, score_scale, up_scale, gate_scale, alpha_attention, alpha_feedforward, cotangent):
    params = tuple((array.astype(jnp.float32) for array in (w_query, w_key, w_value, w_out, w_up, w_gate, w_down, score_scale, up_scale, gate_scale, alpha_attention, alpha_feedforward)))
    hidden = hidden_in.astype(jnp.float32).reshape(N_DP, SEQ, D)
    doc_rows = doc_index.reshape(N_DP, SEQ)
    positions = doc_position.reshape(N_DP, SEQ)

    def forward(weights, inputs):

        def one_sequence(pieces):
            return block_forward(weights, pieces[0], pieces[1], pieces[2])
        return lax.map(jax.checkpoint(one_sequence), (inputs, doc_rows, positions))
    output, pullback = jax.vjp(forward, params, hidden)
    grad_params, grad_hidden = pullback(cotangent.astype(jnp.float32).reshape(N_DP, SEQ, D))
    return (output.reshape(TOKENS, D).astype(jnp.bfloat16), grad_hidden.reshape(TOKENS, D), grad_params[0], grad_params[1], grad_params[2], grad_params[3], grad_params[4], grad_params[5], grad_params[6], grad_params[7], grad_params[8], grad_params[9], grad_params[10], grad_params[11])
```

```python
from functools import partial

import jax
import jax.numpy as jnp
from jax import lax
from jax.experimental import pallas as pl
from jax.experimental.layout import Layout, with_layout_constraint
from jax.experimental.pallas import tpu as pltpu
from jax.sharding import PartitionSpec as P

HEAD_DIM = 64
HALF = HEAD_DIM // 2
BLOCK = 256
EPSILON = 1e-06
LOG2E = 1.4426950408889634
FILL = 20_000_000_000
BF = jnp.bfloat16
F32 = jnp.float32


def swap(value, bit, size, name="mp"):
    return lax.ppermute(value, name, [(i, i ^ bit) for i in range(size)])


def gather_start(own, size):
    blocks = {0: own}
    bit = size // 2
    while bit > 1:
        blocks.update({b ^ bit: swap(v, bit, size) for b, v in list(blocks.items())})
        bit //= 2
    return {b: v for b, v in blocks.items() if b}


def gather_finish(blocks, done, size, order=None, own=None):
    if order is not None:
        blocks = {b: order.fill(own, v) for b, v in blocks.items()}
    blocks = {b: after(v, done) for b, v in blocks.items()}
    for b, v in list(blocks.items()):
        got = swap(v, 1, size)
        blocks[b ^ 1] = got if order is None else order.fill(v, got)
    return [blocks[b] for b in range(2, size)]


def add_low(left, right):
    return (left.astype(F32) + right.astype(F32)).astype(BF)


def scatter_far(far, size, order=None):
    sums = {}
    for b in range(size - 2, 1, -2):
        got = swap(far[b - 1], 1, size)
        if order is not None:
            got = order.fill(far[b - 1], got)
        sums[b] = add_low(far[b - 2], got)
    terms = []
    bit = 2
    while bit < size:
        kept = {}
        for b in sorted(sums, reverse=True):
            if not b & bit:
                kept[b] = add_low(sums[b], swap(sums[b ^ bit], bit, size))
            elif b == bit:
                sent = sums[b]
                terms.append(swap(sent, bit, size))
        sums = kept
        bit *= 2
    return terms, sent


def after(value, done):
    return lax.optimization_barrier((value, done))[0]


def stand_in_kernel(mark_ref, sent_ref, out_ref):
    out_ref[...] = mark_ref[...]


class Order:
    def __init__(self):
        self.last = None
        self.hint = jnp.zeros((8, 128), F32)

    def fill(self, sent, *got):
        tile = pl.BlockSpec((8, 128), lambda i: (0, 0))
        hint = pl.pallas_call(
            stand_in_kernel,
            grid=(1,),
            in_specs=[tile, pl.BlockSpec(memory_space=pl.ANY)],
            out_specs=tile,
            out_shape=jax.ShapeDtypeStruct((8, 128), F32),
            cost_estimate=pl.CostEstimate(flops=FILL, bytes_accessed=0, transcendentals=0),
            name="stand_in",
        )(self.hint, sent)
        *got, self.hint = lax.optimization_barrier((*got, hint))
        return got if len(got) > 1 else got[0]

    def tie(self, *values):
        if self.last is not None:
            values = lax.optimization_barrier((*values, self.last))[:-1]
        return values if len(values) > 1 else values[0]

    def mark(self, value):
        self.last = value
        return value


def take(rows, place, bits, left, other):
    at = (place // bits[0]) % 2
    lead = 1 << left.index(bits[0])
    split = rows.reshape(lead, 2, rows.shape[0] // (2 * lead), rows.shape[1])
    half = lax.dynamic_slice_in_dim(split, 1 - at if other else at, 1, 1)
    return half.reshape(rows.shape[0] // 2, rows.shape[1])


class Reduction:
    def __init__(self, order, grad, bits, place):
        self.order, self.bits, self.place = order, list(bits), place
        self.size = 1 << len(bits)
        self.left = [1 << i for i in reversed(range(len(bits)))]
        self.send([grad])

    def send(self, terms):
        sides = []
        for other in (True, False):
            halves = [take(t, self.place, self.bits, self.left, other) for t in terms]
            sides.append(halves[0] if len(halves) == 1 else add_low(*halves))
        self.held = sides[1]
        self.got = swap(self.order.mark(sides[0]), self.bits[0], self.size, "dp")
        self.left.remove(self.bits.pop(0))

    def step(self):
        held, got = self.order.tie(self.held, self.got)
        if self.bits:
            self.send([held, got])
        else:
            return self.order.mark(held.astype(F32) + got.astype(F32))


VMEM_LIMIT = 56 * 1024 * 1024


def whole_spec(shape):
    return pl.BlockSpec(shape, lambda *_: (0,) * len(shape))


def dot(left, right):
    return jnp.dot(left, right, preferred_element_type=F32)


def dot_tn(left, right):
    return lax.dot_general(left, right, (((0,), (0,)), ((), ())), preferred_element_type=F32)


def dot_nt(left, right):
    return lax.dot_general(left, right, (((1,), (1,)), ((), ())), preferred_element_type=F32)


def cost(*_):
    return pl.CostEstimate(flops=1, bytes_accessed=1, transcendentals=0)


def params():
    return pltpu.CompilerParams(vmem_limit_bytes=VMEM_LIMIT)


def project_kernel(first, count, me_ref, *refs):
    x_refs, refs = refs[:count], refs[count:]
    wq_ref, wk_ref, wv_ref, cos_ref, sin_ref, scale_ref = refs[:6]
    q_ref, k_ref, v_ref, rq_ref, rk_ref = refs[-5:]
    width = q_ref.shape[0]
    heads = width // HEAD_DIM
    scale = scale_ref[...].reshape(heads, 2, HALF, 1)
    for b in range(count):
        here = slice(b * BLOCK, (b + 1) * BLOCK)
        x = x_refs[b][...]
        at = pl.ds(pl.multiple_of((me_ref[0] ^ (first + b)) * BLOCK, BLOCK), BLOCK)
        cos, sin = cos_ref[:, at][None], sin_ref[:, at][None]
        for w_ref, o_ref, r_ref in ((wq_ref, q_ref, rq_ref), (wk_ref, k_ref, rk_ref)):
            pairs = dot(x, w_ref[...]).T.reshape(heads, 2, HALF, BLOCK)
            one, two = pairs[:, 0], pairs[:, 1]
            ra, rb = one * cos - two * sin, two * cos + one * sin
            square = jnp.sum(ra * ra + rb * rb, axis=1, keepdims=True) * (1.0 / HEAD_DIM)
            r = lax.rsqrt(square + EPSILON)
            r_ref[:, :, here] = r
            out = jnp.stack([ra * r * scale[:, 0], rb * r * scale[:, 1]], axis=1)
            o_ref[:, here] = out.reshape(width, BLOCK).astype(BF)
        v_ref[:, here] = dot(x, wv_ref[...]).T.astype(BF)


def project(me, first, blocks, held, wq, wk, wv, cos, sin, scale):
    count = len(blocks)
    seq = cos.shape[1]
    depth, width = wq.shape
    heads = width // HEAD_DIM
    place = first // count
    tall = pl.BlockSpec((width, count * BLOCK), lambda i, me: (0, place))
    row = pl.BlockSpec((heads, 1, count * BLOCK), lambda i, me: (0, 0, place))
    held = list(held)
    return pl.pallas_call(
        partial(project_kernel, first, count),
        grid_spec=pltpu.PrefetchScalarGridSpec(
            num_scalar_prefetch=1,
            grid=(1,),
            in_specs=[whole_spec((BLOCK, depth))] * count
            + [whole_spec((depth, width))] * 3
            + [whole_spec((HALF, seq))] * 2
            + [whole_spec((width, 1))]
            + [pl.BlockSpec(memory_space=pl.ANY)] * len(held),
            out_specs=[tall, tall, tall, row, row],
        ),
        out_shape=[jax.ShapeDtypeStruct((width, seq), BF)] * 3
        + [jax.ShapeDtypeStruct((heads, 1, seq), F32)] * 2,
        input_output_aliases={count + 7 + i: i for i in range(len(held))},
        compiler_params=params(),
        cost_estimate=cost(6 * count * BLOCK * depth * width, 2 * count * BLOCK * depth + 6 * depth * width),
        name="project",
    )(me, *blocks, wq, wk, wv, cos, sin, scale, *held)


def block_at(me, index):
    return pl.ds(pl.multiple_of((me ^ index) * BLOCK, BLOCK), BLOCK)


def allowed(start, low, first, diagonal):
    key = lax.broadcasted_iota(jnp.int32, (BLOCK, BLOCK), 0)
    seen = key >= start - first
    if diagonal:
        seen = seen & (key <= lax.broadcasted_iota(jnp.int32, (BLOCK, BLOCK), 1))
    return seen


def attend_kernel(me_ref, q_ref, k_ref, v_ref, start_ref, o_ref, l_ref, kn_ref):
    me = me_ref[0]
    blocks = q_ref.shape[1] // BLOCK
    factor = LOG2E / HEAD_DIM**0.5
    for j in range(blocks):
        kn_ref[j * BLOCK : (j + 1) * BLOCK, :] = k_ref[:, block_at(me, j)].T
    for i in range(blocks):
        here = block_at(me, i)
        q = q_ref[:, here]
        start = start_ref[:, i * BLOCK : (i + 1) * BLOCK]
        total = jnp.zeros((1, BLOCK), F32)
        out = jnp.zeros((HEAD_DIM, BLOCK), F32)
        for j in range(i + 1):
            s = jnp.dot(kn_ref[j * BLOCK : (j + 1) * BLOCK, :], q, preferred_element_type=F32)
            p = jnp.where(allowed(start, i, j * BLOCK, i == j), jnp.exp2(s * factor), 0.0)
            total = total + jnp.sum(p, axis=0, keepdims=True)
            out = out + jnp.dot(v_ref[:, block_at(me, j)], p.astype(BF), preferred_element_type=F32)
        o_ref[:, here] = (out / total).astype(BF)
        l_ref[0, :, here] = jnp.log2(total)


def attend(me, q, k, v, start):
    width, seq = q.shape
    heads = width // HEAD_DIM
    head = pl.BlockSpec((HEAD_DIM, seq), lambda h, me: (h, 0))
    row = pl.BlockSpec((1, 1, seq), lambda h, me: (h, 0, 0))
    return pl.pallas_call(
        attend_kernel,
        grid_spec=pltpu.PrefetchScalarGridSpec(
            num_scalar_prefetch=1,
            grid=(heads,),
            in_specs=[head, head, head, pl.BlockSpec((1, seq), lambda h, me: (0, 0))],
            out_specs=[head, row],
            scratch_shapes=[pltpu.VMEM((seq, HEAD_DIM), BF)],
        ),
        out_shape=[
            jax.ShapeDtypeStruct((width, seq), BF),
            jax.ShapeDtypeStruct((heads, 1, seq), F32),
        ],
        cost_estimate=pl.CostEstimate(
            flops=8 * seq * seq * width, bytes_accessed=8 * seq * width, transcendentals=heads * seq * seq // 2
        ),
        compiler_params=params(),
        name="attend",
    )(me, q, k, v, start)


PAIR = 2 * HEAD_DIM


def attend_back_kernel(
    me_ref, q_ref, k_ref, v_ref, o_ref, do_ref, l_ref, start_ref, rq_ref, rk_ref, cos_ref, sin_ref, scale_ref,
    g_ref, gs_ref, qn_ref, kn_ref, vn_ref, dn_ref, dq_ref,
):
    me = me_ref[0]
    blocks = q_ref.shape[1] // BLOCK
    factor = LOG2E / HEAD_DIM**0.5
    scale = scale_ref[...]

    def rows(j):
        return slice(j * BLOCK, (j + 1) * BLOCK)

    for j in range(blocks):
        here = block_at(me, j)
        qn_ref[rows(j), :] = q_ref[:, here].T
        kn_ref[rows(j), :] = k_ref[:, here].T
        vn_ref[rows(j), :] = v_ref[:, here].T
        dn_ref[rows(j), :] = do_ref[:, here].T

    def prepare_back(grad, value, r_ref, j):
        at = block_at(me, j)
        unit = value.astype(F32) / scale
        grad = grad * (1.0 / HEAD_DIM**0.5)
        share = jnp.sum(unit * grad, axis=1, keepdims=True)
        g = grad * scale
        cos, sin = cos_ref[:, rows(j)], sin_ref[:, rows(j)]
        out = []
        for h in range(2):
            head = slice(h * HEAD_DIM, (h + 1) * HEAD_DIM)
            inner = jnp.sum(unit[head] * g[head], axis=0, keepdims=True) * (1.0 / HEAD_DIM)
            part = (g[head] - unit[head] * inner) * r_ref[h, :, at]
            one, two = part[:HALF], part[HALF:]
            out += [one * cos + two * sin, two * cos - one * sin]
        return jnp.concatenate(out, axis=0).T.astype(BF), share

    total_share = jnp.zeros((PAIR, 1), F32)
    for j in range(blocks):
        at_j = block_at(me, j)
        dks, dvs = [], []
        for h in range(2):
            head = slice(h * HEAD_DIM, (h + 1) * HEAD_DIM)
            kn, vn, kt = kn_ref[rows(j), head], vn_ref[rows(j), head], k_ref[head, at_j]
            dk = jnp.zeros((BLOCK, HEAD_DIM), F32)
            dv = jnp.zeros((BLOCK, HEAD_DIM), F32)
            for i in range(j, blocks):
                at_i = block_at(me, i)
                do = do_ref[head, at_i]
                delta = jnp.sum(do.astype(F32) * o_ref[head, at_i].astype(F32), axis=0, keepdims=True)
                s = dot(kn, q_ref[head, at_i])
                p = jnp.exp2(s * factor - l_ref[h, :, at_i])
                p = jnp.where(allowed(start_ref[:, rows(i)], i, j * BLOCK, i == j), p, 0.0)
                ds = (p * (dot(vn, do) - delta)).astype(BF)
                dv = dv + dot(p.astype(BF), dn_ref[rows(i), head])
                dk = dk + dot(ds, qn_ref[rows(i), head])
                dq = dot(kt, ds)
                if j == 0:
                    dq_ref[head, rows(i)] = dq
                else:
                    dq_ref[head, rows(i)] += dq
            dks.append(dk)
            dvs.append(dv)
        g_ref[at_j, 2 * PAIR :] = jnp.concatenate(dvs, axis=1).astype(BF)
        out, share = prepare_back(jnp.concatenate(dks, axis=1).T, k_ref[:, at_j], rk_ref, j)
        g_ref[at_j, PAIR : 2 * PAIR] = out
        total_share = total_share + share
        out, share = prepare_back(dq_ref[:, rows(j)], q_ref[:, at_j], rq_ref, j)
        g_ref[at_j, :PAIR] = out
        total_share = total_share + share
    gs_ref[...] = total_share


def attend_back(which, me, q, k, v, o, do, l, start, rq, rk, cos, sin, scale):
    seq = q.shape[1]
    pair = pl.BlockSpec((PAIR, seq), lambda i, me: (which, 0))
    row = pl.BlockSpec((2, 1, seq), lambda i, me: (which, 0, 0))
    return pl.pallas_call(
        attend_back_kernel,
        grid_spec=pltpu.PrefetchScalarGridSpec(
            num_scalar_prefetch=1,
            grid=(1,),
            in_specs=[pair] * 5
            + [row, whole_spec((1, seq)), row, row, whole_spec((HALF, seq)), whole_spec((HALF, seq))]
            + [pl.BlockSpec((PAIR, 1), lambda i, me: (which, 0))],
            out_specs=[whole_spec((seq, 3 * PAIR)), whole_spec((PAIR, 1))],
            scratch_shapes=[pltpu.VMEM((seq, PAIR), BF)] * 4 + [pltpu.VMEM((PAIR, seq), F32)],
        ),
        out_shape=[jax.ShapeDtypeStruct((seq, 3 * PAIR), BF), jax.ShapeDtypeStruct((PAIR, 1), F32)],
        compiler_params=params(),
        cost_estimate=cost(20 * seq * seq * PAIR, 16 * seq * PAIR, seq * seq),
        name="attend_back",
    )(me, q, k, v, o, do, l, start, rq, rk, cos, sin, scale)


def root_mean(values):
    return lax.rsqrt(jnp.mean(values * values, axis=-1, keepdims=True) + EPSILON)


def sum_refs(refs):
    total = refs[0][...].astype(F32)
    for ref in refs[1:]:
        total = total + ref[...].astype(F32)
    return total


def row_call(kernel, name, blocks, vectors, outs):
    depth = blocks[0].shape[1]
    return pl.pallas_call(
        kernel,
        grid=(1,),
        in_specs=[whole_spec((BLOCK, depth))] * len(blocks) + [whole_spec(t.shape) for t in vectors],
        out_specs=[whole_spec((rows, depth)) for _, rows in outs],
        out_shape=[jax.ShapeDtypeStruct((rows, depth), t) for t, rows in outs],
        compiler_params=params(),
        cost_estimate=cost(),
        name=name,
    )(*blocks, *vectors)


def middle_update(terms, x, alpha):
    n = len(terms)

    def kernel(*refs):
        x_ref, alpha_ref, mid_ref, low_ref = refs[n:]
        mixed = sum_refs(refs[:n])
        x = x_ref[...].astype(F32)
        stepped = x + alpha_ref[...] * (mixed * root_mean(mixed) - x)
        middle = stepped * root_mean(stepped)
        mid_ref[...] = middle
        low_ref[...] = middle.astype(BF)

    return row_call(kernel, "middle_update", [*terms, x], [alpha], [(F32, BLOCK), (BF, BLOCK)])


def step_back(base, mixed, alpha, grad):
    r_mixed = root_mean(mixed)
    unit = mixed * r_mixed
    apart = unit - base
    stepped = base + alpha * apart
    r = root_mean(stepped)
    value = stepped * r
    grad_step = r * (grad - value * jnp.mean(value * grad, axis=-1, keepdims=True))
    grad_unit = alpha * grad_step
    grad_mixed = r_mixed * (grad_unit - unit * jnp.mean(unit * grad_unit, axis=-1, keepdims=True))
    share = jnp.sum(grad_step * apart, axis=0, keepdims=True)
    return value, grad_step - grad_unit, grad_mixed, share


def last_update(terms, middle, cotangent, alpha):
    n = len(terms)

    def kernel(*refs):
        mid_ref, cot_ref, alpha_ref, out_ref, res_ref, low_ref, share_ref = refs[n:]
        value, res, grad_mixed, share = step_back(
            mid_ref[...], sum_refs(refs[:n]), alpha_ref[...], cot_ref[...].astype(F32)
        )
        out_ref[...] = value.astype(BF)
        res_ref[...] = res
        low_ref[...] = grad_mixed.astype(BF)
        share_ref[...] = share

    return row_call(kernel, "last_update", [*terms, middle, cotangent], [alpha], [(BF, BLOCK), (F32, BLOCK), (BF, BLOCK), (F32, 1)])


def input_update(terms, grad, hint):
    n = len(terms)

    def kernel(*refs):
        grad_ref, hint_ref, out_ref = refs[n:]
        out_ref[...] = sum_refs(refs[:n]) + grad_ref[...]

    return row_call(kernel, "input_update", [*terms, grad], [hint], [(F32, BLOCK)])[0]


def middle_back(terms, x, grads, grad_res, alpha):
    n, m = len(terms), len(grads)

    def kernel(*refs):
        x_ref, res_ref, alpha_ref, out_ref, low_ref, share_ref = refs[n + m :]
        grad = sum_refs(refs[n : n + m]) + res_ref[...]
        _, res, grad_mixed, share = step_back(
            x_ref[...].astype(F32), sum_refs(refs[:n]), alpha_ref[...], grad
        )
        out_ref[...] = res
        low_ref[...] = grad_mixed.astype(BF)
        share_ref[...] = share

    return row_call(kernel, "middle_back", [*terms, *grads, x, grad_res], [alpha], [(F32, BLOCK), (BF, BLOCK), (F32, 1)])


def body(
    n_mp, x_bits, z_bits,
    hidden_in, doc_index, doc_position, w_query, w_key, w_value, w_out, w_up, w_gate, w_down,
    score_scale, up_scale, gate_scale, alpha_attention, alpha_feedforward, cotangent,
):
    depth, width = w_query.shape
    seq = doc_position.shape[0]
    me = lax.axis_index("mp").astype(jnp.int32).reshape(1)
    place = lax.axis_index("dp").astype(jnp.int32)
    x_first = x_bits + z_bits
    z_first = z_bits[:1] + x_bits + z_bits[1:]
    n_dp = 1 << len(x_first)

    tokens = jnp.arange(seq, dtype=jnp.int32)
    start = (tokens - doc_position).reshape(1, seq)
    steps = jnp.arange(HALF).astype(F32)
    inverse = jnp.exp(steps * (-2.0 * jnp.log(10000.0) / HEAD_DIM))
    angles = inverse[:, None] * doc_position.astype(F32)[None, :]
    cos, sin = jnp.cos(angles), jnp.sin(angles)
    scale = score_scale.reshape(width, 1)
    alpha_attention = alpha_attention.reshape(1, depth)
    alpha_feedforward = alpha_feedforward.reshape(1, depth)
    up_scale, gate_scale = up_scale.reshape(1, -1), gate_scale.reshape(1, -1)
    far_count = n_mp - 2

    def join(blocks):
        return jnp.concatenate(blocks, axis=0)

    def cut(parts):
        return [parts[b * BLOCK : (b + 1) * BLOCK] for b in range(parts.shape[0] // BLOCK)]

    near = slice(0, 2 * BLOCK)
    rest = slice(2 * BLOCK, None)
    pairs = range(width // PAIR)

    def columns(w, i):
        return w[:, i * PAIR : (i + 1) * PAIR]

    w_pairs = [jnp.concatenate([columns(w, i) for w in (w_query, w_key, w_value)], axis=1) for i in pairs]

    coming = gather_start(hidden_in, n_mp)
    x_near = [hidden_in, swap(hidden_in, 1, n_mp)]
    held = project(me, 0, x_near, [], w_query, w_key, w_value, cos, sin, scale)
    x_far = gather_finish(coming, held[0], n_mp)
    for i in range(0, far_count, 2):
        held = project(me, 2 + i, x_far[i : i + 2], held, w_query, w_key, w_value, cos, sin, scale)
    q, k, v, rq, rk = held
    o, l = attend(me, q, k, v, start)
    far_terms, sent = scatter_far(cut(dot_tn(o[:, rest], w_out).astype(BF)), n_mp)
    parts = cut(dot_tn(after(o, sent)[:, near], w_out).astype(BF))
    attn_terms = [parts[0], swap(parts[1], 1, n_mp), *far_terms]
    middle, middle_low = middle_update(attn_terms, hidden_in, alpha_attention)

    def unit(rows):
        u = dot(rows, w_up)
        g = dot(rows, w_gate)
        gate = g * gate_scale
        inner = (u * up_scale * (gate / (1.0 + jnp.exp(-gate)))).astype(BF)
        return u.astype(BF), g.astype(BF), inner, dot(inner, w_down).astype(BF)

    coming = gather_start(middle_low, n_mp)
    mid_near = join([middle_low, swap(middle_low, 1, n_mp)])
    u0, g0, inner0, parts = unit(mid_near)
    mid_far = join(gather_finish(coming, parts, n_mp))
    u1, g1, inner1, far = unit(mid_far)
    far_terms, sent = scatter_far(cut(far), n_mp)
    parts = cut(after(parts, sent))
    mid_all, inner_all, x_all = lax.optimization_barrier(
        tuple(jnp.concatenate(t, axis=0) for t in ([mid_near, after(mid_far, sent)], [inner0, inner1], x_near + x_far))
    )
    ff_terms = [parts[0], swap(parts[1], 1, n_mp), *far_terms]
    layer_out, grad_res, grad_low, share_ff = last_update(ff_terms, middle, cotangent, alpha_feedforward)

    def unit_back(rows, u, g):
        grad = dot_nt(rows, w_down)
        u, g = u.astype(F32), g.astype(F32)
        gate = g * gate_scale
        sig = 1.0 / (1.0 + jnp.exp(-gate))
        by_up = grad * (gate * sig)
        by_gate = grad * (u * up_scale) * (sig * (1.0 + gate * (1.0 - sig)))
        du, dg = (by_up * up_scale).astype(BF), (by_gate * gate_scale).astype(BF)
        shares = jnp.stack([jnp.sum(by_up * u, axis=0), jnp.sum(by_gate * g, axis=0)])
        return du, dg, shares

    def unit_parts(du, dg):
        return (dot_nt(du, w_up) + dot_nt(dg, w_gate)).astype(BF)

    order = Order()
    coming = gather_start(grad_low, n_mp)
    g_near = [grad_low, swap(grad_low, 1, n_mp)]
    du0, dg0, shares0 = unit_back(join(g_near), u0, g0)
    near_parts = order.mark(unit_parts(du0, dg0))
    g_far = gather_finish(coming, near_parts, n_mp)
    g_all = join(g_near + g_far)
    grad_down = Reduction(order, dot_tn(g_all, inner_all).astype(BF), x_first, place)
    du1, dg1, shares1 = unit_back(order.tie(g_all)[2 * BLOCK :], u1, g1)
    far = unit_parts(du1, dg1)
    far_terms, sent = scatter_far(cut(far), n_mp, order)
    order.mark(sent)
    unit_scales = shares0 + shares1

    def over_tokens(near, far):
        return dot_tn(mid_all, jnp.concatenate([near, order.tie(far)], axis=0)).astype(BF)

    grad_gate = Reduction(order, over_tokens(dg0, dg1), z_first, place)
    grad_up = Reduction(order, over_tokens(du0, du1), x_first, place)
    parts = cut(order.tie(near_parts))
    mid_terms = [parts[0], swap(parts[1], 1, n_mp), *far_terms]
    mid_terms[-1] = order.fill(sent, order.tie(mid_terms[-1]))
    grad_x, grad_low, share_attn = middle_back(attn_terms, hidden_in, mid_terms, grad_res, alpha_attention)
    order.mark(grad_low)

    coming = gather_start(grad_low, n_mp)
    a_near = [grad_low, swap(grad_low, 1, n_mp)]
    do_near = order.mark(dot_nt(w_out, order.tie(join(a_near))).astype(BF))
    grad_down.step()
    a_far = gather_finish(coming, order.last, n_mp, order, grad_low)
    do = order.mark(jnp.concatenate([do_near, dot_nt(w_out, join(a_far)).astype(BF)], axis=1))
    a_all = join(a_near + a_far)
    grad_gate.step()
    grad_up.step()

    def rows_first(grad):
        return with_layout_constraint(grad.astype(BF), Layout(major_to_minor=(0, 1)))

    shares = jnp.concatenate([share_attn, share_ff], axis=0).reshape(2, n_mp, -1)
    shares = [lax.dynamic_index_in_dim(shares, me[0] ^ b, 1, keepdims=False).astype(BF) for b in range(n_mp)]
    alpha = [shares[0], swap(shares[1], 1, n_mp)]
    far_shares = [swap(t, 1, n_mp) if b % 2 else t for b, t in enumerate(shares[2:])]
    g_pairs, s_pairs, joints = [], [], []

    def rows_first(grad):
        return with_layout_constraint(grad.astype(BF), Layout(major_to_minor=(0, 1)))

    for i in pairs:
        g_pair, s_pair = attend_back(i, me, q, k, v, o, order.tie(do), l, start, rq, rk, cos, sin, scale)
        order.mark(g_pair)
        g_pairs.append(g_pair)
        s_pairs.append(s_pair)
        if i == 0:
            far_shares = order.tie(*far_shares, *alpha)
            alpha, far_shares = list(far_shares[-2:]), far_shares[:-2]
            far_shares = [add_low(*far_shares[b : b + 2]) for b in range(0, far_count, 2)]
            sums = {2 * b + 2: t for b, t in enumerate(far_shares)}
            bit = 2
            while bit < n_mp:
                alpha.append(swap(sums.pop(bit), bit, n_mp))
                for b in [b for b in sums if b & bit]:
                    sums[b ^ bit] = add_low(sums[b ^ bit], swap(sums.pop(b), bit, n_mp))
                bit *= 2
            for reduction in (grad_down, grad_gate, grad_up):
                reduction.step()
        if i == pairs[-1]:
            far_pairs = [order.tie(g)[rest] for g in g_pairs]
            total = sum(dot_nt(g, w) for g, w in zip(far_pairs, w_pairs))
            far_terms, sent = scatter_far(cut(total.astype(BF)), n_mp, order)
            order.mark(sent)
            alpha = sum(t.astype(F32) for t in order.tie(*alpha))
            small = [jnp.concatenate(s_pairs)[:, 0], unit_scales[0], unit_scales[1], *alpha]
            lengths = [t.shape[0] // n_dp for t in small]
            extra = jnp.concatenate([t.reshape(n_dp, 1, -1) for t in small], axis=2).astype(BF)
            columns = 3 * PAIR + (width if i == 0 else 0)
            extra = jnp.pad(extra, ((0, 0), (0, 15), (0, columns - extra.shape[2])))
        grads = [rows_first(dot_tn(order.tie(x_all), g_pair))]
        if i == 0:
            grad_out = lax.dot_general(a_all, order.tie(o), (((0,), (1,)), ((), ())), preferred_element_type=F32)
            grads.append(rows_first(grad_out))
        grads = jnp.concatenate(grads, axis=1)
        if i == pairs[-1]:
            grads = jnp.concatenate([grads.reshape(n_dp, -1, columns), extra], axis=1).reshape(-1, columns)
        joints.append(Reduction(order, grads, x_first, place))
        order.mark(grads)

    def finish(reduction):
        while reduction.bits:
            reduction.step()
        return reduction.step()

    order.mark(sent)
    joints[0].step()
    bulk = []
    for reduction in (grad_gate, grad_up, grad_down):
        order.mark(sent)
        bulk.append(finish(reduction))
    grad_gate, grad_up, grad_down = bulk
    order.mark(sent)
    near_pairs = [order.tie(g)[near] for g in g_pairs]
    total = sum(dot_nt(g, w) for g, w in zip(near_pairs, w_pairs))
    parts = cut(order.mark(total.astype(BF)))
    in_terms = [parts[0], swap(parts[1], 1, n_mp), *far_terms]
    for reduction in joints[::-1]:
        reduction.step()
    in_terms[-1] = order.fill(sent, order.tie(in_terms[-1]))
    grad_input = input_update(in_terms, grad_x, order.hint)
    order.mark(grad_input)
    joints[-1].step()
    joints = [finish(reduction) for reduction in joints]
    ends = [sum(lengths[: i + 1]) for i in range(len(lengths))]
    extra, joints[-1] = joints[-1][-16], joints[-1][:-16]
    score, up_share, gate_share, alpha_a, alpha_f = [extra[e - n : e] for e, n in zip(ends, lengths)]
    grad_query, grad_key, grad_value = [
        jnp.concatenate([joint[:, i * PAIR : (i + 1) * PAIR] for joint in joints], axis=1) for i in range(3)
    ]
    grad_out, grad_down = joints[0][: depth // n_dp, 3 * PAIR :].T, grad_down.T
    return (
        layer_out,
        grad_input,
        grad_query,
        grad_key,
        grad_value,
        grad_out,
        grad_up,
        grad_gate,
        grad_down,
        score,
        up_share,
        gate_share,
        alpha_a,
        alpha_f,
    )


def solution(mesh):
    n_dp, n_mp = mesh.shape["dp"], mesh.shape["mp"]
    bits = [1 << i for i in range(n_dp.bit_length() - 1)]
    cut = len(bits) // 2
    token = P(("dp", "mp"), None)
    split = P(("mp", "dp"))
    return jax.shard_map(
        partial(body, n_mp, bits[:cut], bits[cut:]),
        mesh=mesh,
        in_specs=(
            token, P("dp"), P("dp"), P(None, "mp"), P(None, "mp"), P(None, "mp"), P("mp", None),
            P(None, "mp"), P(None, "mp"), P("mp", None), P("mp"), P("mp"), P("mp"), P(), P(), token,
        ),
        out_specs=(
            token, token, P("dp", "mp"), P("dp", "mp"), P("dp", "mp"), P("mp", "dp"),
            P("dp", "mp"), P("dp", "mp"), P("mp", "dp"), split, split, split, split, split,
        ),
        check_vma=False,
    )
```

```python
from functools import partial

import jax
import jax.numpy as jnp
from jax import lax
from jax.experimental import pallas as pl
from jax.experimental.layout import Layout, with_layout_constraint
from jax.experimental.pallas import tpu as pltpu
from jax.sharding import PartitionSpec as P

HEAD_DIM = 64
HALF = HEAD_DIM // 2
BLOCK = 256
EPSILON = 1e-06
LOG2E = 1.4426950408889634
FILL = 20_000_000_000
BF = jnp.bfloat16
F32 = jnp.float32


def swap(value, bit, size, name="mp"):
    return lax.ppermute(value, name, [(i, i ^ bit) for i in range(size)])


def gather_start(own, size):
    blocks = {0: own}
    bit = size // 2
    while bit > 1:
        blocks.update({b ^ bit: swap(v, bit, size) for b, v in list(blocks.items())})
        bit //= 2
    return {b: v for b, v in blocks.items() if b}


def gather_finish(blocks, done, size, order=None, own=None):
    blocks = {b: after(v, done) for b, v in blocks.items()}
    if order is not None:
        blocks = {b: order.fill(own, v) for b, v in blocks.items()}
    for b, v in list(blocks.items()):
        got = swap(v, 1, size)
        blocks[b ^ 1] = got if order is None else order.fill(v, got)
    return [blocks[b] for b in range(2, size)]


def add_low(left, right):
    return (left.astype(F32) + right.astype(F32)).astype(BF)


def scatter_far(far, size, order=None):
    sums = {}
    for b in range(size - 2, 1, -2):
        got = swap(far[b - 1], 1, size)
        if order is not None:
            got = order.fill(far[b - 1], got)
        sums[b] = add_low(far[b - 2], got)
    terms = []
    bit = 2
    while bit < size:
        kept = {}
        for b in sorted(sums, reverse=True):
            if not b & bit:
                kept[b] = add_low(sums[b], swap(sums[b ^ bit], bit, size))
            elif b == bit:
                sent = sums[b]
                terms.append(swap(sent, bit, size))
        sums = kept
        bit *= 2
    return terms, sent


def after(value, done):
    return lax.optimization_barrier((value, done))[0]


def stand_in_kernel(mark_ref, sent_ref, out_ref):
    out_ref[...] = mark_ref[...]


class Order:
    def __init__(self):
        self.last = None
        self.hint = jnp.zeros((8, 128), F32)

    def fill(self, sent, *got):
        tile = pl.BlockSpec((8, 128), lambda i: (0, 0))
        hint = pl.pallas_call(
            stand_in_kernel,
            grid=(1,),
            in_specs=[tile, pl.BlockSpec(memory_space=pl.ANY)],
            out_specs=tile,
            out_shape=jax.ShapeDtypeStruct((8, 128), F32),
            cost_estimate=pl.CostEstimate(flops=FILL, bytes_accessed=0, transcendentals=0),
            name="stand_in",
        )(self.hint, sent)
        *got, self.hint = lax.optimization_barrier((*got, hint))
        return got if len(got) > 1 else got[0]

    def tie(self, *values):
        if self.last is not None:
            values = lax.optimization_barrier((*values, self.last))[:-1]
        return values if len(values) > 1 else values[0]

    def mark(self, value):
        self.last = value
        return value


def take(rows, place, bits, left, other):
    at = (place // bits[0]) % 2
    lead = 1 << left.index(bits[0])
    split = rows.reshape(lead, 2, rows.shape[0] // (2 * lead), rows.shape[1])
    half = lax.dynamic_slice_in_dim(split, 1 - at if other else at, 1, 1)
    return half.reshape(rows.shape[0] // 2, rows.shape[1])


class Reduction:
    def __init__(self, order, grads, bits, place):
        self.order, self.bits, self.place = order, list(bits), place
        self.size = 1 << len(bits)
        self.left = [1 << i for i in reversed(range(len(bits)))]
        self.send([[t] for t in grads])

    def send(self, sums):
        sides = []
        for other in (True, False):
            halves = [[take(t, self.place, self.bits, self.left, other) for t in terms] for terms in sums]
            sides.append([t[0] if len(t) == 1 else add_low(*t) for t in halves])
        self.held = sides[1]
        part = sides[0][0] if len(sides[0]) == 1 else jnp.concatenate(sides[0], axis=0)
        self.got = swap(self.order.mark(part), self.bits[0], self.size, "dp")
        self.left.remove(self.bits.pop(0))

    def arrived(self):
        *held, got = self.order.tie(*self.held, self.got)
        sums, row = [], 0
        for t in held:
            sums.append([t, got[row : row + t.shape[0]]])
            row += t.shape[0]
        return sums

    def step(self):
        self.send(self.arrived())

    def merge(self, others):
        sums = self.arrived()
        for reduction in others:
            sums += reduction.arrived()
        self.send(sums)

    def finish(self):
        while self.bits:
            self.step()
        return self.arrived()


VMEM_LIMIT = 56 * 1024 * 1024


def whole_spec(shape):
    return pl.BlockSpec(shape, lambda *_: (0,) * len(shape))


def dot(left, right):
    return jnp.dot(left, right, preferred_element_type=F32)


def dot_tn(left, right):
    return lax.dot_general(left, right, (((0,), (0,)), ((), ())), preferred_element_type=F32)


def dot_nt(left, right):
    return lax.dot_general(left, right, (((1,), (1,)), ((), ())), preferred_element_type=F32)


def cost(*_):
    return pl.CostEstimate(flops=1, bytes_accessed=1, transcendentals=0)


def params():
    return pltpu.CompilerParams(vmem_limit_bytes=VMEM_LIMIT)


def project_kernel(first, count, me_ref, *refs):
    x_refs, refs = refs[:count], refs[count:]
    wq_ref, wk_ref, wv_ref, cos_ref, sin_ref, scale_ref = refs[:6]
    q_ref, k_ref, v_ref, rq_ref, rk_ref = refs[-5:]
    width = q_ref.shape[0]
    heads = width // HEAD_DIM
    scale = scale_ref[...].reshape(heads, 2, HALF, 1)
    for b in range(count):
        here = slice(b * BLOCK, (b + 1) * BLOCK)
        x = x_refs[b][...]
        at = pl.ds(pl.multiple_of((me_ref[0] ^ (first + b)) * BLOCK, BLOCK), BLOCK)
        cos, sin = cos_ref[:, at][None], sin_ref[:, at][None]
        for w_ref, o_ref, r_ref in ((wq_ref, q_ref, rq_ref), (wk_ref, k_ref, rk_ref)):
            pairs = dot(x, w_ref[...]).T.reshape(heads, 2, HALF, BLOCK)
            one, two = pairs[:, 0], pairs[:, 1]
            ra, rb = one * cos - two * sin, two * cos + one * sin
            square = jnp.sum(ra * ra + rb * rb, axis=1, keepdims=True) * (1.0 / HEAD_DIM)
            r = lax.rsqrt(square + EPSILON)
            r_ref[:, :, here] = r
            out = jnp.stack([ra * r * scale[:, 0], rb * r * scale[:, 1]], axis=1)
            o_ref[:, here] = out.reshape(width, BLOCK).astype(BF)
        v_ref[:, here] = dot(x, wv_ref[...]).T.astype(BF)


def project(me, first, blocks, held, wq, wk, wv, cos, sin, scale):
    count = len(blocks)
    seq = cos.shape[1]
    depth, width = wq.shape
    heads = width // HEAD_DIM
    place = first // count
    tall = pl.BlockSpec((width, count * BLOCK), lambda i, me: (0, place))
    row = pl.BlockSpec((heads, 1, count * BLOCK), lambda i, me: (0, 0, place))
    held = list(held)
    return pl.pallas_call(
        partial(project_kernel, first, count),
        grid_spec=pltpu.PrefetchScalarGridSpec(
            num_scalar_prefetch=1,
            grid=(1,),
            in_specs=[whole_spec((BLOCK, depth))] * count
            + [whole_spec((depth, width))] * 3
            + [whole_spec((HALF, seq))] * 2
            + [whole_spec((width, 1))]
            + [pl.BlockSpec(memory_space=pl.ANY)] * len(held),
            out_specs=[tall, tall, tall, row, row],
        ),
        out_shape=[jax.ShapeDtypeStruct((width, seq), BF)] * 3
        + [jax.ShapeDtypeStruct((heads, 1, seq), F32)] * 2,
        input_output_aliases={count + 7 + i: i for i in range(len(held))},
        compiler_params=params(),
        cost_estimate=cost(6 * count * BLOCK * depth * width, 2 * count * BLOCK * depth + 6 * depth * width),
        name="project",
    )(me, *blocks, wq, wk, wv, cos, sin, scale, *held)


def block_at(me, index):
    return pl.ds(pl.multiple_of((me ^ index) * BLOCK, BLOCK), BLOCK)


def allowed(start, low, first, diagonal):
    key = lax.broadcasted_iota(jnp.int32, (BLOCK, BLOCK), 0)
    seen = key >= start - first
    if diagonal:
        seen = seen & (key <= lax.broadcasted_iota(jnp.int32, (BLOCK, BLOCK), 1))
    return seen


def attend_kernel(me_ref, q_ref, k_ref, v_ref, start_ref, o_ref, l_ref, kn_ref):
    me = me_ref[0]
    width, seq = q_ref.shape
    blocks = seq // BLOCK
    factor = LOG2E / HEAD_DIM**0.5
    for j in range(blocks):
        kn_ref[j * BLOCK : (j + 1) * BLOCK, :] = k_ref[:, block_at(me, j)].T
    for i in range(blocks):
        here = block_at(me, i)
        start = start_ref[:, i * BLOCK : (i + 1) * BLOCK]
        masks = [allowed(start, i, j * BLOCK, i == j) for j in range(i + 1)]
        heads = [slice(h * HEAD_DIM, (h + 1) * HEAD_DIM) for h in range(width // HEAD_DIM)]
        totals = [jnp.zeros((1, BLOCK), F32) for _ in heads]
        outs = [jnp.zeros((HEAD_DIM, BLOCK), F32) for _ in heads]
        for j in range(i + 1):
            scores = [dot(kn_ref[j * BLOCK : (j + 1) * BLOCK, head], q_ref[head, here]) for head in heads]
            probs = [jnp.where(masks[j], jnp.exp2(s * factor), 0.0) for s in scores]
            totals = [t + jnp.sum(p, axis=0, keepdims=True) for t, p in zip(totals, probs)]
            outs = [
                t + dot(v_ref[head, block_at(me, j)], p.astype(BF)) for t, head, p in zip(outs, heads, probs)
            ]
        for h, head in enumerate(heads):
            o_ref[head, here] = (outs[h] * (1.0 / totals[h])).astype(BF)
            l_ref[h, :, here] = jnp.log2(totals[h])


def attend(me, q, k, v, start):
    width, seq = q.shape
    heads = width // HEAD_DIM
    tall = whole_spec((width, seq))
    return pl.pallas_call(
        attend_kernel,
        grid_spec=pltpu.PrefetchScalarGridSpec(
            num_scalar_prefetch=1,
            grid=(1,),
            in_specs=[tall, tall, tall, whole_spec((1, seq))],
            out_specs=[tall, whole_spec((heads, 1, seq))],
            scratch_shapes=[pltpu.VMEM((seq, width), BF)],
        ),
        out_shape=[jax.ShapeDtypeStruct((width, seq), BF), jax.ShapeDtypeStruct((heads, 1, seq), F32)],
        compiler_params=params(),
        cost_estimate=cost(),
        name="attend",
    )(me, q, k, v, start)


PAIR = 2 * HEAD_DIM
GROUP = 2


def attend_back_kernel(
    me_ref, q_ref, k_ref, v_ref, o_ref, do_ref, l_ref, start_ref, rq_ref, rk_ref, cos_ref, sin_ref, scale_ref,
    g_ref, gs_ref, qn_ref, kn_ref, vn_ref, dn_ref, dq_ref, delta_ref,
):
    me = me_ref[0]
    width, seq = q_ref.shape
    blocks = seq // BLOCK
    heads = width // HEAD_DIM
    factor = LOG2E / HEAD_DIM**0.5
    scale = scale_ref[...]

    def rows(j):
        return slice(j * BLOCK, (j + 1) * BLOCK)

    for j in range(blocks):
        here = block_at(me, j)
        qn_ref[rows(j), :] = q_ref[:, here].T
        kn_ref[rows(j), :] = k_ref[:, here].T
        vn_ref[rows(j), :] = v_ref[:, here].T
        dn_ref[rows(j), :] = do_ref[:, here].T
        both = do_ref[:, here].astype(F32) * o_ref[:, here].astype(F32)
        for h in range(heads):
            head = slice(h * HEAD_DIM, (h + 1) * HEAD_DIM)
            delta_ref[h, :, rows(j)] = jnp.sum(both[head], axis=0, keepdims=True)

    def prepare_back(grad, value, r_ref, j, n):
        at = block_at(me, j)
        unit = value.astype(F32) / scale
        grad = grad * (1.0 / HEAD_DIM**0.5)
        gs_ref[...] += jnp.sum(unit * grad, axis=1, keepdims=True)
        g = grad * scale
        cos, sin = cos_ref[:, rows(j)], sin_ref[:, rows(j)]
        out = []
        for h in range(heads):
            head = slice(h * HEAD_DIM, (h + 1) * HEAD_DIM)
            inner = jnp.sum(unit[head] * g[head], axis=0, keepdims=True) * (1.0 / HEAD_DIM)
            part = (g[head] - unit[head] * inner) * r_ref[h, :, at]
            one, two = part[:HALF], part[HALF:]
            out += [one * cos + two * sin, two * cos - one * sin]
        for p in range(width // PAIR):
            pair = jnp.concatenate(out[4 * p : 4 * p + 4], axis=0).T.astype(BF)
            g_ref[at, (3 * p + n) * PAIR : (3 * p + n + 1) * PAIR] = pair

    gs_ref[...] = jnp.zeros_like(gs_ref)
    for j in range(blocks):
        at_j = block_at(me, j)
        masks = [allowed(start_ref[:, rows(i)], i, j * BLOCK, i == j) for i in range(j, blocks)]
        dks = [jnp.zeros((BLOCK, HEAD_DIM), F32) for _ in range(heads)]
        dvs = list(dks)
        for first in range(0, heads, GROUP):
            group = [(h, slice(h * HEAD_DIM, (h + 1) * HEAD_DIM)) for h in range(first, min(first + GROUP, heads))]
            for i in range(j, blocks):
                at_i = block_at(me, i)
                scores = [dot(kn_ref[rows(j), head], q_ref[head, at_i]) for _, head in group]
                dps = [dot(vn_ref[rows(j), head], do_ref[head, at_i]) for _, head in group]
                ps = [
                    jnp.where(masks[i - j], jnp.exp2(s * factor - l_ref[h, :, at_i]), 0.0)
                    for (h, _), s in zip(group, scores)
                ]
                dss = [
                    (p * (dp - delta_ref[h, :, rows(i)])).astype(BF) for (h, _), p, dp in zip(group, ps, dps)
                ]
                for (h, head), p, ds in zip(group, ps, dss):
                    dvs[h] = dvs[h] + dot(p.astype(BF), dn_ref[rows(i), head])
                    dks[h] = dks[h] + dot(ds, qn_ref[rows(i), head])
                    dq = dot(k_ref[head, at_j], ds)
                    if j == 0:
                        dq_ref[head, rows(i)] = dq
                    else:
                        dq_ref[head, rows(i)] += dq
        for p in range(width // PAIR):
            pair = jnp.concatenate(dvs[2 * p : 2 * p + 2], axis=1).astype(BF)
            g_ref[at_j, (3 * p + 2) * PAIR : (3 * p + 3) * PAIR] = pair
        prepare_back(jnp.concatenate(dks, axis=1).T, k_ref[:, at_j], rk_ref, j, 1)
        prepare_back(dq_ref[:, rows(j)], q_ref[:, at_j], rq_ref, j, 0)


def attend_back(me, q, k, v, o, do, l, start, rq, rk, cos, sin, scale):
    width, seq = q.shape
    heads = width // HEAD_DIM
    row = whole_spec((heads, 1, seq))
    return pl.pallas_call(
        attend_back_kernel,
        grid_spec=pltpu.PrefetchScalarGridSpec(
            num_scalar_prefetch=1,
            grid=(1,),
            in_specs=[whole_spec((width, seq))] * 5
            + [row, whole_spec((1, seq)), row, row, whole_spec((HALF, seq)), whole_spec((HALF, seq))]
            + [whole_spec((width, 1))],
            out_specs=[whole_spec((seq, 3 * width)), whole_spec((width, 1))],
            scratch_shapes=[pltpu.VMEM((seq, width), BF)] * 4
            + [pltpu.VMEM((width, seq), F32), pltpu.VMEM((heads, 1, seq), F32)],
        ),
        out_shape=[jax.ShapeDtypeStruct((seq, 3 * width), BF), jax.ShapeDtypeStruct((width, 1), F32)],
        compiler_params=params(),
        cost_estimate=cost(),
        name="attend_back",
    )(me, q, k, v, o, do, l, start, rq, rk, cos, sin, scale)


def root_mean(values):
    return lax.rsqrt(jnp.mean(values * values, axis=-1, keepdims=True) + EPSILON)


def sum_refs(refs):
    total = refs[0][...].astype(F32)
    for ref in refs[1:]:
        total = total + ref[...].astype(F32)
    return total


ROWS = 128


def row_call(kernel, name, blocks, vectors, outs):
    depth = blocks[0].shape[1]
    tile = pl.BlockSpec((ROWS, depth), lambda i: (i, 0))
    return pl.pallas_call(
        kernel,
        grid=(BLOCK // ROWS,),
        in_specs=[tile] * len(blocks) + [whole_spec(t.shape) for t in vectors],
        out_specs=[tile if rows == BLOCK else whole_spec((rows, depth)) for _, rows in outs],
        out_shape=[jax.ShapeDtypeStruct((rows, depth), t) for t, rows in outs],
        compiler_params=params(),
        cost_estimate=cost(),
        name=name,
    )(*blocks, *vectors)


def middle_update(terms, x, alpha):
    n = len(terms)

    def kernel(*refs):
        x_ref, alpha_ref, mid_ref, low_ref = refs[n:]
        mixed = sum_refs(refs[:n])
        x = x_ref[...].astype(F32)
        stepped = x + alpha_ref[...] * (mixed * root_mean(mixed) - x)
        middle = stepped * root_mean(stepped)
        mid_ref[...] = middle
        low_ref[...] = middle.astype(BF)

    return row_call(kernel, "middle_update", [*terms, x], [alpha], [(F32, BLOCK), (BF, BLOCK)])


def step_back(base, mixed, alpha, grad):
    r_mixed = root_mean(mixed)
    unit = mixed * r_mixed
    apart = unit - base
    stepped = base + alpha * apart
    r = root_mean(stepped)
    value = stepped * r
    grad_step = r * (grad - value * jnp.mean(value * grad, axis=-1, keepdims=True))
    grad_unit = alpha * grad_step
    grad_mixed = r_mixed * (grad_unit - unit * jnp.mean(unit * grad_unit, axis=-1, keepdims=True))
    share = jnp.sum(grad_step * apart, axis=0, keepdims=True)
    return value, grad_step - grad_unit, grad_mixed, share


def add_share(share_ref, share):
    @pl.when(pl.program_id(0) == 0)
    def _():
        share_ref[...] = share

    @pl.when(pl.program_id(0) > 0)
    def _():
        share_ref[...] += share


def last_update(terms, middle, cotangent, alpha):
    n = len(terms)

    def kernel(*refs):
        mid_ref, cot_ref, alpha_ref, out_ref, res_ref, low_ref, share_ref = refs[n:]
        value, res, grad_mixed, share = step_back(
            mid_ref[...], sum_refs(refs[:n]), alpha_ref[...], cot_ref[...].astype(F32)
        )
        out_ref[...] = value.astype(BF)
        res_ref[...] = res
        low_ref[...] = grad_mixed.astype(BF)
        add_share(share_ref, share)

    return row_call(kernel, "last_update", [*terms, middle, cotangent], [alpha], [(BF, BLOCK), (F32, BLOCK), (BF, BLOCK), (F32, 1)])


def joint_sums(ends, width):
    rows, extra = ends[0][0].shape[0], ends[0][1].shape[0]

    def kernel(*refs):
        ins, outs = refs[: 3 * len(ends)], refs[3 * len(ends) :]
        for i in range(len(ends)):
            held_ref, small_ref, got_ref = ins[3 * i : 3 * i + 3]
            total = held_ref[...].astype(F32) + got_ref[:rows, :].astype(F32)
            for n, out_ref in enumerate(outs[:3]):
                out_ref[:, i * PAIR : (i + 1) * PAIR] = total[:, n * PAIR : (n + 1) * PAIR]
            outs[3][i * PAIR : (i + 1) * PAIR, :] = total[:, 3 * PAIR :].T
        outs[4][...] = small_ref[...].astype(F32) + got_ref[rows:, :].astype(F32)

    return pl.pallas_call(
        kernel,
        out_shape=[jax.ShapeDtypeStruct((rows, width), F32)] * 3
        + [jax.ShapeDtypeStruct((width, rows), F32), jax.ShapeDtypeStruct((extra, 4 * PAIR), F32)],
        compiler_params=params(),
        cost_estimate=cost(),
        name="joint_sums",
    )(*[t for end in ends for t in end])


def input_update(terms, grad, hint):
    n = len(terms)

    def kernel(*refs):
        grad_ref, hint_ref, out_ref = refs[n:]
        out_ref[...] = sum_refs(refs[:n]) + grad_ref[...]

    return row_call(kernel, "input_update", [*terms, grad], [hint], [(F32, BLOCK)])[0]


def middle_back(terms, x, grads, grad_res, alpha):
    n, m = len(terms), len(grads)

    def kernel(*refs):
        x_ref, res_ref, alpha_ref, out_ref, low_ref, share_ref = refs[n + m :]
        grad = sum_refs(refs[n : n + m]) + res_ref[...]
        _, res, grad_mixed, share = step_back(
            x_ref[...].astype(F32), sum_refs(refs[:n]), alpha_ref[...], grad
        )
        out_ref[...] = res
        low_ref[...] = grad_mixed.astype(BF)
        add_share(share_ref, share)

    return row_call(kernel, "middle_back", [*terms, *grads, x, grad_res], [alpha], [(F32, BLOCK), (BF, BLOCK), (F32, 1)])


def body(
    n_mp, x_bits, z_bits,
    hidden_in, doc_index, doc_position, w_query, w_key, w_value, w_out, w_up, w_gate, w_down,
    score_scale, up_scale, gate_scale, alpha_attention, alpha_feedforward, cotangent,
):
    depth, width = w_query.shape
    seq = doc_position.shape[0]
    me = lax.axis_index("mp").astype(jnp.int32).reshape(1)
    place = lax.axis_index("dp").astype(jnp.int32)
    x_first = x_bits + z_bits
    z_first = z_bits[:1] + x_bits + z_bits[1:]
    n_dp = 1 << len(x_first)

    tokens = jnp.arange(seq, dtype=jnp.int32)
    start = (tokens - doc_position).reshape(1, seq)
    steps = jnp.arange(HALF).astype(F32)
    inverse = jnp.exp(steps * (-2.0 * jnp.log(10000.0) / HEAD_DIM))
    angles = inverse[:, None] * doc_position.astype(F32)[None, :]
    cos, sin = jnp.cos(angles), jnp.sin(angles)
    scale = score_scale.reshape(width, 1)
    alpha_attention = alpha_attention.reshape(1, depth)
    alpha_feedforward = alpha_feedforward.reshape(1, depth)
    up_scale, gate_scale = up_scale.reshape(1, -1), gate_scale.reshape(1, -1)
    far_count = n_mp - 2

    def join(blocks):
        return jnp.concatenate(blocks, axis=0)

    def cut(parts):
        return [parts[b * BLOCK : (b + 1) * BLOCK] for b in range(parts.shape[0] // BLOCK)]

    near = slice(0, 2 * BLOCK)
    rest = slice(2 * BLOCK, None)
    pairs = range(width // PAIR)

    def columns(w, i):
        return w[:, i * PAIR : (i + 1) * PAIR]

    w_joint = jnp.concatenate(
        [columns(w, i) for i in pairs for w in (w_query, w_key, w_value)], axis=1
    )

    coming = gather_start(hidden_in, n_mp)
    x_near = [hidden_in, swap(hidden_in, 1, n_mp)]
    held = project(me, 0, x_near, [], w_query, w_key, w_value, cos, sin, scale)
    x_far = gather_finish(coming, held[0], n_mp)
    for i in range(0, far_count, 2):
        held = project(me, 2 + i, x_far[i : i + 2], held, w_query, w_key, w_value, cos, sin, scale)
    q, k, v, rq, rk = held
    o, l = attend(me, q, k, v, start)
    far_terms, sent = scatter_far(cut(dot_tn(o[:, rest], w_out).astype(BF)), n_mp)
    parts = cut(dot_tn(after(o, sent)[:, near], w_out).astype(BF))
    attn_terms = [parts[0], swap(parts[1], 1, n_mp), *far_terms]
    middle, middle_low = middle_update(attn_terms, hidden_in, alpha_attention)

    def unit(rows):
        u = dot(rows, w_up)
        g = dot(rows, w_gate)
        gate = g * gate_scale
        inner = (u * up_scale * (gate / (1.0 + jnp.exp(-gate)))).astype(BF)
        return u.astype(BF), g.astype(BF), inner, dot(inner, w_down).astype(BF)

    coming = gather_start(middle_low, n_mp)
    mid_near = join([middle_low, swap(middle_low, 1, n_mp)])
    u0, g0, inner0, parts = unit(mid_near)
    mid_far = join(gather_finish(coming, parts, n_mp))
    u1, g1, inner1, far = unit(mid_far)
    far_terms, sent = scatter_far(cut(far), n_mp)
    parts = cut(after(parts, sent))
    mid_all, inner_all, x_all = (
        jnp.concatenate(t, axis=0) for t in ([mid_near, after(mid_far, sent)], [inner0, after(inner1, sent)], x_near + x_far)
    )
    ff_terms = [parts[0], swap(parts[1], 1, n_mp), *far_terms]
    ff_terms[-1], mid_all, inner_all, x_all = lax.optimization_barrier((ff_terms[-1], mid_all, inner_all, x_all))
    layer_out, grad_res, grad_low, share_ff = last_update(ff_terms, middle, cotangent, alpha_feedforward)

    def unit_back(rows, u, g):
        grad = dot_nt(rows, w_down)
        u, g = u.astype(F32), g.astype(F32)
        gate = g * gate_scale
        sig = 1.0 / (1.0 + jnp.exp(-gate))
        by_up = grad * (gate * sig)
        by_gate = grad * (u * up_scale) * (sig * (1.0 + gate * (1.0 - sig)))
        du, dg = (by_up * up_scale).astype(BF), (by_gate * gate_scale).astype(BF)
        shares = jnp.stack([jnp.sum(by_up * u, axis=0), jnp.sum(by_gate * g, axis=0)])
        return du, dg, shares

    def unit_parts(du, dg):
        return (dot_nt(du, w_up) + dot_nt(dg, w_gate)).astype(BF)

    order = Order()
    coming = gather_start(grad_low, n_mp)
    g_near = [grad_low, order.fill(grad_low, swap(grad_low, 1, n_mp))]
    du0, dg0, shares0 = unit_back(join(g_near), u0, g0)
    near_parts = order.mark(unit_parts(du0, dg0))
    g_far = gather_finish(coming, near_parts, n_mp)
    g_all = join(g_near + g_far)
    grad_down = Reduction(order, [dot_tn(g_all, inner_all).astype(BF)], x_first, place)
    du1, dg1, shares1 = unit_back(order.tie(g_all)[2 * BLOCK :], u1, g1)
    far = unit_parts(du1, dg1)
    far_terms, sent = scatter_far(cut(far), n_mp, order)
    order.mark(sent)
    unit_scales = shares0 + shares1

    def over_tokens(near, far):
        return dot_tn(mid_all, jnp.concatenate([near, order.tie(far)], axis=0)).astype(BF)

    grad_gate = Reduction(order, [over_tokens(dg0, dg1)], z_first, place)
    grad_up = Reduction(order, [over_tokens(du0, du1)], x_first, place)
    parts = cut(order.tie(near_parts))
    mid_terms = [parts[0], swap(parts[1], 1, n_mp), *far_terms]
    mid_terms[-1] = order.fill(sent, order.tie(mid_terms[-1]))
    grad_x, grad_low, share_attn = middle_back(attn_terms, hidden_in, mid_terms, grad_res, alpha_attention)
    order.mark(grad_low)

    coming = gather_start(grad_low, n_mp)
    a_near = [grad_low, swap(grad_low, 1, n_mp)]
    do_near = order.mark(dot_nt(w_out, order.tie(join(a_near))).astype(BF))
    grad_down.step()
    grad_gate.step()
    a_far = gather_finish(coming, order.last, n_mp, order, grad_low)
    do = order.mark(jnp.concatenate([do_near, dot_nt(w_out, join(a_far)).astype(BF)], axis=1))
    a_all = join(a_near + a_far)
    grad_up.step()

    def rows_first(grad):
        return with_layout_constraint(grad.astype(BF), Layout(major_to_minor=(0, 1)))

    grad_joint, grad_scale = attend_back(me, q, k, v, o, order.tie(do), l, start, rq, rk, cos, sin, scale)
    order.mark(grad_joint)
    grad_out = lax.dot_general(a_all, order.tie(o), (((0,), (1,)), ((), ())), preferred_element_type=F32)
    grad_out = rows_first(grad_out)
    shares = jnp.concatenate([share_attn, share_ff], axis=0).reshape(2 * n_mp, n_dp, -1)
    early = [shares.transpose(1, 0, 2), unit_scales.reshape(2, n_dp, -1).transpose(1, 0, 2)]
    joints = []
    for i in pairs:
        grads = rows_first(dot_tn(order.tie(x_all), grad_joint[:, 3 * i * PAIR : 3 * (i + 1) * PAIR]))
        grads = jnp.concatenate([grads, columns(grad_out, i)], axis=1)
        small = early if i == 0 else []
        if i == pairs[-1]:
            small = small + [grad_scale.reshape(1, n_dp, -1).transpose(1, 0, 2)]
        small = jnp.concatenate([t.reshape(n_dp, 1, -1) for t in small], axis=2).astype(BF)
        small = jnp.pad(small, ((0, 0), (0, 15), (0, 4 * PAIR - small.shape[2]))).reshape(-1, 4 * PAIR)
        joints.append(Reduction(order, [grads, small], z_first if i % 2 else x_first, place))
    while len(grad_up.bits) > 1:
        for reduction in (grad_up, grad_gate, grad_down):
            reduction.step()
    grad_up.merge([grad_gate, grad_down])
    far = dot_nt(order.tie(grad_joint)[rest], w_joint).astype(BF)
    far_terms, sent = scatter_far(cut(far), n_mp, order)
    order.mark(sent)
    joints[0].step()
    parts = cut(dot_nt(order.tie(grad_joint)[near], w_joint).astype(BF))
    order.mark(parts[1])
    in_terms = [parts[0], swap(parts[1], 1, n_mp), *far_terms]
    for reduction in joints:
        while len(reduction.bits) > 1:
            reduction.step()
    in_terms[-1] = order.fill(sent, order.tie(in_terms[-1]))
    grad_input = input_update(in_terms, grad_x, order.hint)
    order.mark(grad_input)
    for reduction in joints:
        reduction.step()
    order.mark(grad_input)
    grad_up, grad_gate, grad_down = [h.astype(F32) + g.astype(F32) for h, g in grad_up.finish()]
    order.mark(grad_input)
    while joints[0].bits:
        for reduction in joints:
            reduction.step()
    ends = [order.tie(*reduction.held, reduction.got) for reduction in joints]
    small = [ends[0][1][0].astype(F32) + ends[0][2][depth // n_dp].astype(F32)]
    shares = small[0][: 2 * n_mp * (depth // n_mp // n_dp)].reshape(2, n_mp, -1)
    shares = [lax.dynamic_index_in_dim(shares, me[0] ^ b, 1, keepdims=False).astype(BF) for b in range(n_mp)]
    alpha = shares[0].astype(F32)
    pieces = {b: t for b, t in enumerate(shares) if b}
    bit = n_mp // 2
    while bit:
        for b in [b for b in list(pieces) if b & bit and b != bit]:
            pieces[b ^ bit] = add_low(pieces[b ^ bit], swap(pieces.pop(b), bit, n_mp))
        alpha = alpha + swap(pieces.pop(bit), bit, n_mp).astype(F32)
        bit //= 2
    scale_rows = small[0][shares[0].shape[1] * 2 * n_mp :]
    count = w_up.shape[1] // n_dp
    up_share, gate_share, score = scale_rows[:count], scale_rows[count : 2 * count], scale_rows[2 * count :]
    alpha_a, alpha_f = alpha[0], alpha[1]
    grad_query, grad_key, grad_value, grad_out, last = joint_sums(ends, width)
    score = (score if len(joints) == 1 else last[0])[: width // n_dp]
    grad_down = grad_down.T
    return (
        layer_out,
        grad_input,
        grad_query,
        grad_key,
        grad_value,
        grad_out,
        grad_up,
        grad_gate,
        grad_down,
        score,
        up_share,
        gate_share,
        alpha_a,
        alpha_f,
    )


def solution(mesh):
    n_dp, n_mp = mesh.shape["dp"], mesh.shape["mp"]
    bits = [1 << i for i in range(n_dp.bit_length() - 1)]
    cut = len(bits) // 2
    token = P(("dp", "mp"), None)
    split = P(("mp", "dp"))
    return jax.shard_map(
        partial(body, n_mp, bits[:cut], bits[cut:]),
        mesh=mesh,
        in_specs=(
            token, P("dp"), P("dp"), P(None, "mp"), P(None, "mp"), P(None, "mp"), P("mp", None),
            P(None, "mp"), P(None, "mp"), P("mp", None), P("mp"), P("mp"), P("mp"), P(), P(), token,
        ),
        out_specs=(
            token, token, P("dp", "mp"), P("dp", "mp"), P("dp", "mp"), P("mp", "dp"),
            P("dp", "mp"), P("dp", "mp"), P("mp", "dp"), split, split, split, split, split,
        ),
        check_vma=False,
    )
```

```python
from functools import partial

import jax
import jax.numpy as jnp
from jax import lax
from jax.experimental import pallas as pl
from jax.experimental.layout import Layout, with_layout_constraint
from jax.experimental.pallas import tpu as pltpu
from jax.sharding import PartitionSpec as P

HEAD_DIM = 64
HALF = HEAD_DIM // 2
BLOCK = 256
EPSILON = 1e-06
LOG2E = 1.4426950408889634
FILL = 20_000_000_000
BF = jnp.bfloat16
F32 = jnp.float32


def swap(value, bit, size, name="mp"):
    return lax.ppermute(value, name, [(i, i ^ bit) for i in range(size)])


def gather_start(own, size):
    blocks = {0: own}
    bit = size // 2
    while bit > 1:
        blocks.update({b ^ bit: swap(v, bit, size) for b, v in list(blocks.items())})
        bit //= 2
    return {b: v for b, v in blocks.items() if b}


def gather_finish(blocks, done, size, order=None, own=None):
    blocks = {b: after(v, done) for b, v in blocks.items()}
    if order is not None:
        blocks = {b: order.fill(own, v) for b, v in blocks.items()}
    for b, v in list(blocks.items()):
        got = swap(v, 1, size)
        blocks[b ^ 1] = got if order is None else order.fill(v, got)
    return [blocks[b] for b in range(2, size)]


def add_low(left, right):
    return (left.astype(F32) + right.astype(F32)).astype(BF)


def scatter_far(far, size, order=None):
    sums = {}
    for b in range(size - 2, 1, -2):
        got = swap(far[b - 1], 1, size)
        if order is not None:
            got = order.fill(far[b - 1], got)
        sums[b] = add_low(far[b - 2], got)
    terms = []
    bit = 2
    while bit < size:
        kept = {}
        for b in sorted(sums, reverse=True):
            if not b & bit:
                kept[b] = add_low(sums[b], swap(sums[b ^ bit], bit, size))
            elif b == bit:
                sent = sums[b]
                terms.append(swap(sent, bit, size))
        sums = kept
        bit *= 2
    return terms, sent


def after(value, done):
    return lax.optimization_barrier((value, done))[0]


def stand_in_kernel(mark_ref, sent_ref, out_ref):
    out_ref[...] = mark_ref[...]


class Order:
    def __init__(self):
        self.last = None
        self.hint = jnp.zeros((8, 128), F32)

    def fill(self, sent, *got):
        tile = pl.BlockSpec((8, 128), lambda i: (0, 0))
        hint = pl.pallas_call(
            stand_in_kernel,
            grid=(1,),
            in_specs=[tile, pl.BlockSpec(memory_space=pl.ANY)],
            out_specs=tile,
            out_shape=jax.ShapeDtypeStruct((8, 128), F32),
            cost_estimate=pl.CostEstimate(flops=FILL, bytes_accessed=0, transcendentals=0),
            name="stand_in",
        )(self.hint, sent)
        *got, self.hint = lax.optimization_barrier((*got, hint))
        return got if len(got) > 1 else got[0]

    def tie(self, *values):
        if self.last is not None:
            values = lax.optimization_barrier((*values, self.last))[:-1]
        return values if len(values) > 1 else values[0]

    def mark(self, value):
        self.last = value
        return value


def take(rows, place, bits, left, other):
    at = (place // bits[0]) % 2
    lead = 1 << left.index(bits[0])
    split = rows.reshape(lead, 2, rows.shape[0] // (2 * lead), rows.shape[1])
    half = lax.dynamic_slice_in_dim(split, 1 - at if other else at, 1, 1)
    return half.reshape(rows.shape[0] // 2, rows.shape[1])


class Reduction:
    def __init__(self, order, grads, bits, place):
        self.order, self.bits, self.place = order, list(bits), place
        self.size = 1 << len(bits)
        self.left = [1 << i for i in reversed(range(len(bits)))]
        self.send([[t] for t in grads])

    def send(self, sums):
        sides = [[take(t, self.place, self.bits, self.left, other) for (t,) in sums] for other in (True, False)]
        part = sides[0][0] if len(sums) == 1 else jnp.concatenate(sides[0], axis=0)
        self.swap(part, sides[1])

    def swap(self, part, held):
        self.held = list(held)
        self.got = swap(self.order.mark(part), self.bits[0], self.size, "dp")
        self.left.remove(self.bits.pop(0))

    def arrived(self):
        *held, got = self.order.tie(*self.held, self.got)
        sums, row = [], 0
        for t in held:
            sums.append([t, got[row : row + t.shape[0]]])
            row += t.shape[0]
        return sums

    def merge(self, others):
        held, gots = [], []
        for reduction in [self, *others]:
            *more, got = self.order.tie(*reduction.held, reduction.got)
            held.append(more)
            gots.append(got)
        bit = self.bits[0]
        side = (self.place // bit) % 2
        self.swap(*sum_sides(held, gots, side.reshape(1), 1 << self.left.index(bit)))

    def step(self):
        self.merge([])

    def finish(self):
        while self.bits:
            self.step()
        return self.arrived()


def sum_sides(held, gots, side, lead):
    flat = [t for group in held for t in group]
    columns = flat[0].shape[1]

    def kernel(side_ref, *refs):
        held_refs, refs = refs[: len(flat)], refs[len(flat) :]
        got_refs, (send_ref, *keep_refs) = refs[: len(gots)], refs[len(gots) :]
        own = side_ref[0]
        row = k = 0
        for group, got_ref in zip(held, got_refs):
            base = 0
            for t in group:
                step = t.shape[0] // (2 * lead)
                for n in range(lead):
                    for out_ref, out_row, at in (
                        (send_ref, row, 2 * n + 1 - own),
                        (keep_refs[k], n * step, 2 * n + own),
                    ):
                        at = pl.multiple_of(at * step, 16)
                        total = held_refs[k][pl.ds(at, step), :].astype(F32)
                        total = total + got_ref[pl.ds(pl.multiple_of(base + at, 16), step), :].astype(F32)
                        out_ref[out_row : out_row + step, :] = total.astype(BF)
                    row += step
                base += t.shape[0]
                k += 1

    send, *keep = pl.pallas_call(
        kernel,
        grid_spec=pltpu.PrefetchScalarGridSpec(
            num_scalar_prefetch=1,
            grid=(1,),
            in_specs=[whole_spec(t.shape) for t in [*flat, *gots]],
            out_specs=[whole_spec((sum(t.shape[0] for t in flat) // 2, columns))]
            + [whole_spec((t.shape[0] // 2, columns)) for t in flat],
        ),
        out_shape=[jax.ShapeDtypeStruct((sum(t.shape[0] for t in flat) // 2, columns), BF)]
        + [jax.ShapeDtypeStruct((t.shape[0] // 2, columns), BF) for t in flat],
        compiler_params=params(),
        cost_estimate=cost(),
        name="sum_sides",
    )(side, *flat, *gots)
    return send, keep


VMEM_LIMIT = 56 * 1024 * 1024


def whole_spec(shape):
    return pl.BlockSpec(shape, lambda *_: (0,) * len(shape))


def dot(left, right):
    return jnp.dot(left, right, preferred_element_type=F32)


def dot_tn(left, right):
    return lax.dot_general(left, right, (((0,), (0,)), ((), ())), preferred_element_type=F32)


def dot_nt(left, right):
    return lax.dot_general(left, right, (((1,), (1,)), ((), ())), preferred_element_type=F32)


def cost(*_):
    return pl.CostEstimate(flops=1, bytes_accessed=1, transcendentals=0)


def params():
    return pltpu.CompilerParams(vmem_limit_bytes=VMEM_LIMIT)


def project_kernel(first, count, me_ref, *refs):
    x_refs, refs = refs[:count], refs[count:]
    wq_ref, wk_ref, wv_ref, cos_ref, sin_ref, scale_ref = refs[:6]
    q_ref, k_ref, v_ref, rq_ref, rk_ref = refs[-5:]
    width = q_ref.shape[0]
    heads = width // HEAD_DIM
    scale = scale_ref[...].reshape(heads, 2, HALF, 1)
    for b in range(count):
        here = slice(b * BLOCK, (b + 1) * BLOCK)
        x = x_refs[b][...]
        at = pl.ds(pl.multiple_of((me_ref[0] ^ (first + b)) * BLOCK, BLOCK), BLOCK)
        cos, sin = cos_ref[:, at][None], sin_ref[:, at][None]
        for w_ref, o_ref, r_ref in ((wq_ref, q_ref, rq_ref), (wk_ref, k_ref, rk_ref)):
            pairs = dot(x, w_ref[...]).T.reshape(heads, 2, HALF, BLOCK)
            one, two = pairs[:, 0], pairs[:, 1]
            ra, rb = one * cos - two * sin, two * cos + one * sin
            square = jnp.sum(ra * ra + rb * rb, axis=1, keepdims=True) * (1.0 / HEAD_DIM)
            r = lax.rsqrt(square + EPSILON)
            r_ref[:, :, here] = r
            out = jnp.stack([ra * r * scale[:, 0], rb * r * scale[:, 1]], axis=1)
            o_ref[:, here] = out.reshape(width, BLOCK).astype(BF)
        v_ref[:, here] = dot(x, wv_ref[...]).T.astype(BF)


def project(me, first, blocks, held, wq, wk, wv, cos, sin, scale):
    count = len(blocks)
    seq = cos.shape[1]
    depth, width = wq.shape
    heads = width // HEAD_DIM
    place = first // count
    tall = pl.BlockSpec((width, count * BLOCK), lambda i, me: (0, place))
    row = pl.BlockSpec((heads, 1, count * BLOCK), lambda i, me: (0, 0, place))
    held = list(held)
    return pl.pallas_call(
        partial(project_kernel, first, count),
        grid_spec=pltpu.PrefetchScalarGridSpec(
            num_scalar_prefetch=1,
            grid=(1,),
            in_specs=[whole_spec((BLOCK, depth))] * count
            + [whole_spec((depth, width))] * 3
            + [whole_spec((HALF, seq))] * 2
            + [whole_spec((width, 1))]
            + [pl.BlockSpec(memory_space=pl.ANY)] * len(held),
            out_specs=[tall, tall, tall, row, row],
        ),
        out_shape=[jax.ShapeDtypeStruct((width, seq), BF)] * 3
        + [jax.ShapeDtypeStruct((heads, 1, seq), F32)] * 2,
        input_output_aliases={count + 7 + i: i for i in range(len(held))},
        compiler_params=params(),
        cost_estimate=cost(6 * count * BLOCK * depth * width, 2 * count * BLOCK * depth + 6 * depth * width),
        name="project",
    )(me, *blocks, wq, wk, wv, cos, sin, scale, *held)


def block_at(me, index):
    return pl.ds(pl.multiple_of((me ^ index) * BLOCK, BLOCK), BLOCK)


def allowed(start, low, first, diagonal):
    key = lax.broadcasted_iota(jnp.int32, (BLOCK, BLOCK), 0)
    seen = key >= start - first
    if diagonal:
        seen = seen & (key <= lax.broadcasted_iota(jnp.int32, (BLOCK, BLOCK), 1))
    return seen


def attend_kernel(me_ref, q_ref, k_ref, v_ref, start_ref, o_ref, l_ref, kn_ref):
    me = me_ref[0]
    width, seq = q_ref.shape
    blocks = seq // BLOCK
    factor = LOG2E / HEAD_DIM**0.5
    for j in range(blocks):
        kn_ref[j * BLOCK : (j + 1) * BLOCK, :] = k_ref[:, block_at(me, j)].T
    for i in range(blocks):
        here = block_at(me, i)
        start = start_ref[:, i * BLOCK : (i + 1) * BLOCK]
        masks = [allowed(start, i, j * BLOCK, i == j) for j in range(i + 1)]
        heads = [slice(h * HEAD_DIM, (h + 1) * HEAD_DIM) for h in range(width // HEAD_DIM)]
        totals = [jnp.zeros((1, BLOCK), F32) for _ in heads]
        outs = [jnp.zeros((HEAD_DIM, BLOCK), F32) for _ in heads]
        for j in range(i + 1):
            scores = [dot(kn_ref[j * BLOCK : (j + 1) * BLOCK, head], q_ref[head, here]) for head in heads]
            probs = [jnp.where(masks[j], jnp.exp2(s * factor), 0.0) for s in scores]
            totals = [t + jnp.sum(p, axis=0, keepdims=True) for t, p in zip(totals, probs)]
            outs = [
                t + dot(v_ref[head, block_at(me, j)], p.astype(BF)) for t, head, p in zip(outs, heads, probs)
            ]
        for h, head in enumerate(heads):
            o_ref[head, here] = (outs[h] * (1.0 / totals[h])).astype(BF)
            l_ref[h, :, here] = jnp.log2(totals[h])


def attend(me, q, k, v, start):
    width, seq = q.shape
    heads = width // HEAD_DIM
    tall = whole_spec((width, seq))
    return pl.pallas_call(
        attend_kernel,
        grid_spec=pltpu.PrefetchScalarGridSpec(
            num_scalar_prefetch=1,
            grid=(1,),
            in_specs=[tall, tall, tall, whole_spec((1, seq))],
            out_specs=[tall, whole_spec((heads, 1, seq))],
            scratch_shapes=[pltpu.VMEM((seq, width), BF)],
        ),
        out_shape=[jax.ShapeDtypeStruct((width, seq), BF), jax.ShapeDtypeStruct((heads, 1, seq), F32)],
        compiler_params=params(),
        cost_estimate=cost(),
        name="attend",
    )(me, q, k, v, start)


PAIR = 2 * HEAD_DIM
GROUP = 2


def attend_back_kernel(
    me_ref, q_ref, k_ref, v_ref, o_ref, do_ref, l_ref, start_ref, rq_ref, rk_ref, cos_ref, sin_ref, scale_ref,
    g_ref, gs_ref, qn_ref, kn_ref, vn_ref, dn_ref, dq_ref, delta_ref,
):
    me = me_ref[0]
    width, seq = q_ref.shape
    blocks = seq // BLOCK
    heads = width // HEAD_DIM
    factor = LOG2E / HEAD_DIM**0.5
    scale = scale_ref[...]

    def rows(j):
        return slice(j * BLOCK, (j + 1) * BLOCK)

    for j in range(blocks):
        here = block_at(me, j)
        qn_ref[rows(j), :] = q_ref[:, here].T
        kn_ref[rows(j), :] = k_ref[:, here].T
        vn_ref[rows(j), :] = v_ref[:, here].T
        dn_ref[rows(j), :] = do_ref[:, here].T
        both = do_ref[:, here].astype(F32) * o_ref[:, here].astype(F32)
        for h in range(heads):
            head = slice(h * HEAD_DIM, (h + 1) * HEAD_DIM)
            delta_ref[h, :, rows(j)] = jnp.sum(both[head], axis=0, keepdims=True)

    def prepare_back(grad, value, r_ref, j, n):
        at = block_at(me, j)
        unit = value.astype(F32) / scale
        grad = grad * (1.0 / HEAD_DIM**0.5)
        gs_ref[...] += jnp.sum(unit * grad, axis=1, keepdims=True)
        g = grad * scale
        cos, sin = cos_ref[:, rows(j)], sin_ref[:, rows(j)]
        out = []
        for h in range(heads):
            head = slice(h * HEAD_DIM, (h + 1) * HEAD_DIM)
            inner = jnp.sum(unit[head] * g[head], axis=0, keepdims=True) * (1.0 / HEAD_DIM)
            part = (g[head] - unit[head] * inner) * r_ref[h, :, at]
            one, two = part[:HALF], part[HALF:]
            out += [one * cos + two * sin, two * cos - one * sin]
        for p in range(width // PAIR):
            pair = jnp.concatenate(out[4 * p : 4 * p + 4], axis=0).T.astype(BF)
            g_ref[at, (3 * p + n) * PAIR : (3 * p + n + 1) * PAIR] = pair

    gs_ref[...] = jnp.zeros_like(gs_ref)
    for j in range(blocks):
        at_j = block_at(me, j)
        masks = [allowed(start_ref[:, rows(i)], i, j * BLOCK, i == j) for i in range(j, blocks)]
        dks = [jnp.zeros((BLOCK, HEAD_DIM), F32) for _ in range(heads)]
        dvs = list(dks)
        for first in range(0, heads, GROUP):
            group = [(h, slice(h * HEAD_DIM, (h + 1) * HEAD_DIM)) for h in range(first, min(first + GROUP, heads))]
            for i in range(j, blocks):
                at_i = block_at(me, i)
                scores = [dot(kn_ref[rows(j), head], q_ref[head, at_i]) for _, head in group]
                dps = [dot(vn_ref[rows(j), head], do_ref[head, at_i]) for _, head in group]
                ps = [
                    jnp.where(masks[i - j], jnp.exp2(s * factor - l_ref[h, :, at_i]), 0.0)
                    for (h, _), s in zip(group, scores)
                ]
                dss = [
                    (p * (dp - delta_ref[h, :, rows(i)])).astype(BF) for (h, _), p, dp in zip(group, ps, dps)
                ]
                for (h, head), p, ds in zip(group, ps, dss):
                    dvs[h] = dvs[h] + dot(p.astype(BF), dn_ref[rows(i), head])
                    dks[h] = dks[h] + dot(ds, qn_ref[rows(i), head])
                    dq = dot(k_ref[head, at_j], ds)
                    if j == 0:
                        dq_ref[head, rows(i)] = dq
                    else:
                        dq_ref[head, rows(i)] += dq
        for p in range(width // PAIR):
            pair = jnp.concatenate(dvs[2 * p : 2 * p + 2], axis=1).astype(BF)
            g_ref[at_j, (3 * p + 2) * PAIR : (3 * p + 3) * PAIR] = pair
        prepare_back(jnp.concatenate(dks, axis=1).T, k_ref[:, at_j], rk_ref, j, 1)
        prepare_back(dq_ref[:, rows(j)], q_ref[:, at_j], rq_ref, j, 0)


def attend_back(me, q, k, v, o, do, l, start, rq, rk, cos, sin, scale):
    width, seq = q.shape
    heads = width // HEAD_DIM
    row = whole_spec((heads, 1, seq))
    return pl.pallas_call(
        attend_back_kernel,
        grid_spec=pltpu.PrefetchScalarGridSpec(
            num_scalar_prefetch=1,
            grid=(1,),
            in_specs=[whole_spec((width, seq))] * 5
            + [row, whole_spec((1, seq)), row, row, whole_spec((HALF, seq)), whole_spec((HALF, seq))]
            + [whole_spec((width, 1))],
            out_specs=[whole_spec((seq, 3 * width)), whole_spec((width, 1))],
            scratch_shapes=[pltpu.VMEM((seq, width), BF)] * 4
            + [pltpu.VMEM((width, seq), F32), pltpu.VMEM((heads, 1, seq), F32)],
        ),
        out_shape=[jax.ShapeDtypeStruct((seq, 3 * width), BF), jax.ShapeDtypeStruct((width, 1), F32)],
        compiler_params=params(),
        cost_estimate=cost(),
        name="attend_back",
    )(me, q, k, v, o, do, l, start, rq, rk, cos, sin, scale)


def root_mean(values):
    return lax.rsqrt(jnp.mean(values * values, axis=-1, keepdims=True) + EPSILON)


def sum_refs(refs):
    total = refs[0][...].astype(F32)
    for ref in refs[1:]:
        total = total + ref[...].astype(F32)
    return total


ROWS = 128


def row_call(kernel, name, blocks, vectors, outs):
    depth = blocks[0].shape[1]
    tile = pl.BlockSpec((ROWS, depth), lambda i: (i, 0))
    return pl.pallas_call(
        kernel,
        grid=(BLOCK // ROWS,),
        in_specs=[tile] * len(blocks) + [whole_spec(t.shape) for t in vectors],
        out_specs=[tile if rows == BLOCK else whole_spec((rows, depth)) for _, rows in outs],
        out_shape=[jax.ShapeDtypeStruct((rows, depth), t) for t, rows in outs],
        compiler_params=params(),
        cost_estimate=cost(),
        name=name,
    )(*blocks, *vectors)


def sum_terms(terms):
    return sum(t.astype(F32) for t in terms)


def middle_update(terms, x, alpha):
    mixed, x = sum_terms(terms), x.astype(F32)
    stepped = x + alpha * (mixed * root_mean(mixed) - x)
    return (stepped * root_mean(stepped)).astype(BF)


def step_back(base, mixed, alpha, grad):
    r_mixed = root_mean(mixed)
    unit = mixed * r_mixed
    apart = unit - base
    stepped = base + alpha * apart
    r = root_mean(stepped)
    value = stepped * r
    grad_step = r * (grad - value * jnp.mean(value * grad, axis=-1, keepdims=True))
    grad_unit = alpha * grad_step
    grad_mixed = r_mixed * (grad_unit - unit * jnp.mean(unit * grad_unit, axis=-1, keepdims=True))
    share = jnp.sum(grad_step * apart, axis=0, keepdims=True)
    return value, grad_step - grad_unit, grad_mixed, share


def add_share(share_ref, share):
    @pl.when(pl.program_id(0) == 0)
    def _():
        share_ref[...] = share

    @pl.when(pl.program_id(0) > 0)
    def _():
        share_ref[...] += share


def last_update(terms, middle, cotangent, alpha):
    n = len(terms)

    def kernel(*refs):
        mid_ref, cot_ref, alpha_ref, out_ref, res_ref, low_ref, share_ref = refs[n:]
        value, res, grad_mixed, share = step_back(
            mid_ref[...].astype(F32), sum_refs(refs[:n]), alpha_ref[...], cot_ref[...].astype(F32)
        )
        out_ref[...] = value.astype(BF)
        res_ref[...] = res.astype(BF)
        low_ref[...] = grad_mixed.astype(BF)
        add_share(share_ref, share)

    return row_call(kernel, "last_update", [*terms, middle, cotangent], [alpha], [(BF, BLOCK), (BF, BLOCK), (BF, BLOCK), (F32, 1)])


def joint_sums(ends, width):
    rows, extra = ends[0][0].shape[0], ends[0][1].shape[0]

    def kernel(*refs):
        ins, outs = refs[: 3 * len(ends)], refs[3 * len(ends) :]
        for i in range(len(ends)):
            held_ref, small_ref, got_ref = ins[3 * i : 3 * i + 3]
            total = held_ref[...].astype(F32) + got_ref[:rows, :].astype(F32)
            for n, out_ref in enumerate(outs[:3]):
                out_ref[:, i * PAIR : (i + 1) * PAIR] = total[:, n * PAIR : (n + 1) * PAIR]
            outs[3][i * PAIR : (i + 1) * PAIR, :] = total[:, 3 * PAIR :].T
        outs[4][...] = small_ref[...].astype(F32) + got_ref[rows:, :].astype(F32)

    return pl.pallas_call(
        kernel,
        out_shape=[jax.ShapeDtypeStruct((rows, width), F32)] * 3
        + [jax.ShapeDtypeStruct((width, rows), F32), jax.ShapeDtypeStruct((extra, 4 * PAIR), F32)],
        compiler_params=params(),
        cost_estimate=cost(),
        name="joint_sums",
    )(*[t for end in ends for t in end])


def input_update(terms, grad, hint):
    n = len(terms)

    def kernel(*refs):
        grad_ref, hint_ref, out_ref = refs[n:]
        out_ref[...] = sum_refs(refs[:n]) + grad_ref[...].astype(F32)

    return row_call(kernel, "input_update", [*terms, grad], [hint], [(F32, BLOCK)])[0]


def middle_back(terms, x, grads, grad_res, alpha):
    grad = sum_terms([*grads, grad_res])
    _, res, grad_mixed, share = step_back(x.astype(F32), sum_terms(terms), alpha, grad)
    return res.astype(BF), grad_mixed.astype(BF), share


def body(
    n_mp, x_bits, z_bits,
    hidden_in, doc_index, doc_position, w_query, w_key, w_value, w_out, w_up, w_gate, w_down,
    score_scale, up_scale, gate_scale, alpha_attention, alpha_feedforward, cotangent,
):
    depth, width = w_query.shape
    seq = doc_position.shape[0]
    me = lax.axis_index("mp").astype(jnp.int32).reshape(1)
    place = lax.axis_index("dp").astype(jnp.int32)
    x_first = x_bits + z_bits
    z_first = z_bits[:1] + x_bits + z_bits[1:]
    n_dp = 1 << len(x_first)

    tokens = jnp.arange(seq, dtype=jnp.int32)
    start = (tokens - doc_position).reshape(1, seq)
    steps = jnp.arange(HALF).astype(F32)
    inverse = jnp.exp(steps * (-2.0 * jnp.log(10000.0) / HEAD_DIM))
    angles = inverse[:, None] * doc_position.astype(F32)[None, :]
    cos, sin = jnp.cos(angles), jnp.sin(angles)
    scale = score_scale.reshape(width, 1)
    alpha_attention = alpha_attention.reshape(1, depth)
    alpha_feedforward = alpha_feedforward.reshape(1, depth)
    up_scale, gate_scale = up_scale.reshape(1, -1), gate_scale.reshape(1, -1)
    far_count = n_mp - 2

    def join(blocks):
        return jnp.concatenate(blocks, axis=0)

    def cut(parts):
        return [parts[b * BLOCK : (b + 1) * BLOCK] for b in range(parts.shape[0] // BLOCK)]

    near = slice(0, 2 * BLOCK)
    rest = slice(2 * BLOCK, None)
    pairs = range(width // PAIR)

    def columns(w, i):
        return w[:, i * PAIR : (i + 1) * PAIR]

    w_joint = jnp.concatenate(
        [columns(w, i) for i in pairs for w in (w_query, w_key, w_value)], axis=1
    )

    coming = gather_start(hidden_in, n_mp)
    x_near = [hidden_in, swap(hidden_in, 1, n_mp)]
    held = project(me, 0, x_near, [], w_query, w_key, w_value, cos, sin, scale)
    x_far = gather_finish(coming, held[0], n_mp)
    for i in range(0, far_count, 2):
        held = project(me, 2 + i, x_far[i : i + 2], held, w_query, w_key, w_value, cos, sin, scale)
    q, k, v, rq, rk = held
    o, l = attend(me, q, k, v, start)
    far_terms, sent = scatter_far(cut(dot_tn(o[:, rest], w_out).astype(BF)), n_mp)
    parts = cut(dot_tn(after(o, sent)[:, near], w_out).astype(BF))
    attn_terms = [parts[0], swap(parts[1], 1, n_mp), *far_terms]
    middle_low = middle_update(attn_terms, hidden_in, alpha_attention)

    def unit(rows):
        u = dot(rows, w_up)
        g = dot(rows, w_gate)
        gate = g * gate_scale
        inner = (u * up_scale * (gate / (1.0 + jnp.exp(-gate)))).astype(BF)
        return u.astype(BF), g.astype(BF), inner, dot(inner, w_down).astype(BF)

    coming = gather_start(middle_low, n_mp)
    mid_near = join([middle_low, swap(middle_low, 1, n_mp)])
    u0, g0, inner0, parts = unit(mid_near)
    mid_far = join(gather_finish(coming, parts, n_mp))
    u1, g1, inner1, far = unit(mid_far)
    far_terms, sent = scatter_far(cut(far), n_mp)
    parts = cut(after(parts, sent))
    mid_all, inner_all, x_all = (
        jnp.concatenate(t, axis=0) for t in ([mid_near, after(mid_far, sent)], [inner0, after(inner1, sent)], x_near + x_far)
    )
    ff_terms = [parts[0], swap(parts[1], 1, n_mp), *far_terms]
    ff_terms[-1], mid_all, inner_all, x_all = lax.optimization_barrier((ff_terms[-1], mid_all, inner_all, x_all))
    layer_out, grad_res, grad_low, share_ff = last_update(ff_terms, middle_low, cotangent, alpha_feedforward)

    def unit_back(rows, u, g):
        grad = dot_nt(rows, w_down)
        u, g = u.astype(F32), g.astype(F32)
        gate = g * gate_scale
        sig = 1.0 / (1.0 + jnp.exp(-gate))
        by_up = grad * (gate * sig)
        by_gate = grad * (u * up_scale) * (sig * (1.0 + gate * (1.0 - sig)))
        du, dg = (by_up * up_scale).astype(BF), (by_gate * gate_scale).astype(BF)
        shares = jnp.stack([jnp.sum(by_up * u, axis=0), jnp.sum(by_gate * g, axis=0)])
        return du, dg, shares

    def unit_parts(du, dg):
        return (dot_nt(du, w_up) + dot_nt(dg, w_gate)).astype(BF)

    order = Order()
    coming = gather_start(grad_low, n_mp)
    g_near = [grad_low, order.fill(grad_low, swap(grad_low, 1, n_mp))]
    du0, dg0, shares0 = unit_back(join(g_near), u0, g0)
    near_parts = order.mark(unit_parts(du0, dg0))
    g_far = gather_finish(coming, near_parts, n_mp)
    g_all = join(g_near + g_far)
    grad_down = Reduction(order, [dot_tn(g_all, inner_all).astype(BF)], x_first, place)
    du1, dg1, shares1 = unit_back(order.tie(g_all)[2 * BLOCK :], u1, g1)
    far = unit_parts(du1, dg1)
    far_terms, sent = scatter_far(cut(far), n_mp, order)
    order.mark(sent)
    unit_scales = shares0 + shares1

    def over_tokens(near, far):
        return dot_tn(mid_all, jnp.concatenate([near, order.tie(far)], axis=0)).astype(BF)

    grad_gate = Reduction(order, [over_tokens(dg0, dg1)], z_first, place)
    grad_up = Reduction(order, [over_tokens(du0, du1)], x_first, place)
    parts = cut(order.tie(near_parts))
    mid_terms = [parts[0], swap(parts[1], 1, n_mp), *far_terms]
    mid_terms[-1] = order.fill(sent, order.tie(mid_terms[-1]))
    grad_x, grad_low, share_attn = middle_back(attn_terms, hidden_in, mid_terms, grad_res, alpha_attention)
    order.mark(grad_low)

    coming = gather_start(grad_low, n_mp)
    a_near = [grad_low, swap(grad_low, 1, n_mp)]
    do_near = order.mark(dot_nt(w_out, order.tie(join(a_near))).astype(BF))
    grad_down.step()
    grad_gate.step()
    a_far = gather_finish(coming, order.last, n_mp, order, grad_low)
    do = order.mark(jnp.concatenate([do_near, dot_nt(w_out, join(a_far)).astype(BF)], axis=1))
    a_all = join(a_near + a_far)
    grad_up.step()

    def rows_first(grad):
        return with_layout_constraint(grad.astype(BF), Layout(major_to_minor=(0, 1)))

    grad_joint, grad_scale = attend_back(me, q, k, v, o, order.tie(do), l, start, rq, rk, cos, sin, scale)
    order.mark(grad_joint)
    grad_out = lax.dot_general(a_all, order.tie(o), (((0,), (1,)), ((), ())), preferred_element_type=F32)
    grad_out = rows_first(grad_out)
    shares = jnp.concatenate([share_attn, share_ff], axis=0).reshape(2 * n_mp, n_dp, -1)
    early = [shares.transpose(1, 0, 2), unit_scales.reshape(2, n_dp, -1).transpose(1, 0, 2)]
    joints = []
    for i in pairs:
        grads = rows_first(dot_tn(order.tie(x_all), grad_joint[:, 3 * i * PAIR : 3 * (i + 1) * PAIR]))
        grads = jnp.concatenate([grads, columns(grad_out, i)], axis=1)
        small = early if i == 0 else []
        if i == pairs[-1]:
            small = small + [grad_scale.reshape(1, n_dp, -1).transpose(1, 0, 2)]
        small = jnp.concatenate([t.reshape(n_dp, 1, -1) for t in small], axis=2).astype(BF)
        small = jnp.pad(small, ((0, 0), (0, 15), (0, 4 * PAIR - small.shape[2]))).reshape(-1, 4 * PAIR)
        joints.append(Reduction(order, [grads, small], z_first if i % 2 else x_first, place))
    while len(grad_up.bits) > 1:
        for reduction in (grad_up, grad_gate, grad_down):
            reduction.step()
    grad_up.merge([grad_gate, grad_down])
    far = dot_nt(order.tie(grad_joint)[rest], w_joint).astype(BF)
    far_terms, sent = scatter_far(cut(far), n_mp, order)
    order.mark(sent)
    joints[0].step()
    parts = cut(dot_nt(order.tie(grad_joint)[near], w_joint).astype(BF))
    order.mark(parts[1])
    in_terms = [parts[0], swap(parts[1], 1, n_mp), *far_terms]
    for reduction in joints:
        while len(reduction.bits) > 1:
            reduction.step()
    in_terms[-1] = order.fill(sent, order.tie(in_terms[-1]))
    grad_input = input_update(in_terms, grad_x, order.hint)
    order.mark(grad_input)
    for reduction in joints:
        reduction.step()
    order.mark(grad_input)
    grad_up, grad_gate, grad_down = [h.astype(F32) + g.astype(F32) for h, g in grad_up.finish()]
    order.mark(grad_input)
    while joints[0].bits:
        for reduction in joints:
            reduction.step()
    ends = [order.tie(*reduction.held, reduction.got) for reduction in joints]
    small = [ends[0][1][0].astype(F32) + ends[0][2][depth // n_dp].astype(F32)]
    shares = small[0][: 2 * n_mp * (depth // n_mp // n_dp)].reshape(2, n_mp, -1)
    shares = [lax.dynamic_index_in_dim(shares, me[0] ^ b, 1, keepdims=False).astype(BF) for b in range(n_mp)]
    alpha = shares[0].astype(F32)
    pieces = {b: t for b, t in enumerate(shares) if b}
    bit = n_mp // 2
    while bit:
        for b in [b for b in list(pieces) if b & bit and b != bit]:
            pieces[b ^ bit] = add_low(pieces[b ^ bit], swap(pieces.pop(b), bit, n_mp))
        alpha = alpha + swap(pieces.pop(bit), bit, n_mp).astype(F32)
        bit //= 2
    scale_rows = small[0][shares[0].shape[1] * 2 * n_mp :]
    count = w_up.shape[1] // n_dp
    up_share, gate_share, score = scale_rows[:count], scale_rows[count : 2 * count], scale_rows[2 * count :]
    alpha_a, alpha_f = alpha[0], alpha[1]
    grad_query, grad_key, grad_value, grad_out, last = joint_sums(ends, width)
    score = (score if len(joints) == 1 else last[0])[: width // n_dp]
    grad_down = grad_down.T
    return (
        layer_out,
        grad_input,
        grad_query,
        grad_key,
        grad_value,
        grad_out,
        grad_up,
        grad_gate,
        grad_down,
        score,
        up_share,
        gate_share,
        alpha_a,
        alpha_f,
    )


def solution(mesh):
    n_dp, n_mp = mesh.shape["dp"], mesh.shape["mp"]
    bits = [1 << i for i in range(n_dp.bit_length() - 1)]
    cut = len(bits) // 2
    token = P(("dp", "mp"), None)
    split = P(("mp", "dp"))
    return jax.shard_map(
        partial(body, n_mp, bits[:cut], bits[cut:]),
        mesh=mesh,
        in_specs=(
            token, P("dp"), P("dp"), P(None, "mp"), P(None, "mp"), P(None, "mp"), P("mp", None),
            P(None, "mp"), P(None, "mp"), P("mp", None), P("mp"), P("mp"), P("mp"), P(), P(), token,
        ),
        out_specs=(
            token, token, P("dp", "mp"), P("dp", "mp"), P("dp", "mp"), P("mp", "dp"),
            P("dp", "mp"), P("dp", "mp"), P("mp", "dp"), split, split, split, split, split,
        ),
        check_vma=False,
    )
```

```python
from functools import partial

import jax
import jax.numpy as jnp
from jax import lax
from jax.experimental import pallas as pl
from jax.experimental.layout import Layout, with_layout_constraint
from jax.experimental.pallas import tpu as pltpu
from jax.sharding import PartitionSpec as P

HEAD_DIM = 64
HALF = HEAD_DIM // 2
BLOCK = 256
EPSILON = 1e-06
LOG2E = 1.4426950408889634
FILL = 20_000_000_000
BF = jnp.bfloat16
F32 = jnp.float32


def swap(value, bit, size, name="mp"):
    return lax.ppermute(value, name, [(i, i ^ bit) for i in range(size)])


def gather_start(own, size):
    blocks = {0: own}
    bit = size // 2
    while bit > 1:
        blocks.update({b ^ bit: swap(v, bit, size) for b, v in list(blocks.items())})
        bit //= 2
    return {b: v for b, v in blocks.items() if b}


def gather_finish(blocks, done, size, order=None, own=None):
    blocks = {b: after(v, done) for b, v in blocks.items()}
    if order is not None:
        blocks = {b: order.fill(own, v) for b, v in blocks.items()}
    for b, v in list(blocks.items()):
        got = swap(v, 1, size)
        blocks[b ^ 1] = got if order is None else order.fill(v, got)
    return [blocks[b] for b in range(2, size)]


def add_low(left, right):
    return (left.astype(F32) + right.astype(F32)).astype(BF)


def scatter_far(far, size, order=None):
    sums = {}
    for b in range(size - 2, 1, -2):
        got = swap(far[b - 1], 1, size)
        if order is not None:
            got = order.fill(far[b - 1], got)
        sums[b] = add_low(far[b - 2], got)
    terms = []
    bit = 2
    while bit < size:
        kept = {}
        for b in sorted(sums, reverse=True):
            if not b & bit:
                kept[b] = add_low(sums[b], swap(sums[b ^ bit], bit, size))
            elif b == bit:
                sent = sums[b]
                terms.append(swap(sent, bit, size))
        sums = kept
        bit *= 2
    return terms, sent


def after(value, done):
    return lax.optimization_barrier((value, done))[0]


def stand_in_kernel(mark_ref, sent_ref, out_ref):
    pass


class Order:
    def __init__(self):
        self.last = None
        self.hint = jnp.zeros((8, 128), F32)

    def fill(self, sent, *got):
        hint = pl.pallas_call(
            stand_in_kernel,
            in_specs=[pl.BlockSpec(memory_space=pl.ANY)] * 2,
            out_specs=pl.BlockSpec(memory_space=pl.ANY),
            out_shape=jax.ShapeDtypeStruct((8, 128), F32),
            input_output_aliases={0: 0},
            cost_estimate=pl.CostEstimate(flops=FILL, bytes_accessed=0, transcendentals=0),
            name="stand_in",
        )(self.hint, sent)
        *got, self.hint = lax.optimization_barrier((*got, hint))
        return got if len(got) > 1 else got[0]

    def tie(self, *values):
        if self.last is not None:
            values = lax.optimization_barrier((*values, self.last))[:-1]
        return values if len(values) > 1 else values[0]

    def mark(self, value):
        self.last = value
        return value


def take(rows, place, bits, left, other):
    at = (place // bits[0]) % 2
    lead = 1 << left.index(bits[0])
    split = rows.reshape(lead, 2, rows.shape[0] // (2 * lead), rows.shape[1])
    half = lax.dynamic_slice_in_dim(split, 1 - at if other else at, 1, 1)
    return half.reshape(rows.shape[0] // 2, rows.shape[1])


class Reduction:
    def __init__(self, order, grads, bits, place):
        self.order, self.bits, self.place = order, list(bits), place
        self.size = 1 << len(bits)
        self.left = [1 << i for i in reversed(range(len(bits)))]
        self.send([[t] for t in grads])

    def send(self, sums):
        sides = [[take(t, self.place, self.bits, self.left, other) for (t,) in sums] for other in (True, False)]
        part = sides[0][0] if len(sums) == 1 else jnp.concatenate(sides[0], axis=0)
        self.swap(part, sides[1])

    def swap(self, part, held):
        self.held = list(held)
        self.got = swap(self.order.mark(part), self.bits[0], self.size, "dp")
        self.left.remove(self.bits.pop(0))

    def arrived(self):
        *held, got = self.order.tie(*self.held, self.got)
        sums, row = [], 0
        for t in held:
            sums.append([t, got[row : row + t.shape[0]]])
            row += t.shape[0]
        return sums

    def merge(self, others):
        held, gots = [], []
        for reduction in [self, *others]:
            *more, got = self.order.tie(*reduction.held, reduction.got)
            held.append(more)
            gots.append(got)
        bit = self.bits[0]
        side = (self.place // bit) % 2
        self.swap(*sum_sides(held, gots, side.reshape(1), 1 << self.left.index(bit)))

    def step(self):
        self.merge([])

    def finish(self):
        while self.bits:
            self.step()
        return self.arrived()


def sum_sides(held, gots, side, lead):
    flat = [t for group in held for t in group]
    columns = flat[0].shape[1]

    def kernel(side_ref, *refs):
        held_refs, refs = refs[: len(flat)], refs[len(flat) :]
        got_refs, (send_ref, *keep_refs) = refs[: len(gots)], refs[len(gots) :]
        own = side_ref[0]
        row = k = 0
        for group, got_ref in zip(held, got_refs):
            base = 0
            for t in group:
                step = t.shape[0] // (2 * lead)
                for n in range(lead):
                    for out_ref, out_row, at in (
                        (send_ref, row, 2 * n + 1 - own),
                        (keep_refs[k], n * step, 2 * n + own),
                    ):
                        at = pl.multiple_of(at * step, 16)
                        total = held_refs[k][pl.ds(at, step), :].astype(F32)
                        total = total + got_ref[pl.ds(pl.multiple_of(base + at, 16), step), :].astype(F32)
                        out_ref[out_row : out_row + step, :] = total.astype(BF)
                    row += step
                base += t.shape[0]
                k += 1

    send, *keep = pl.pallas_call(
        kernel,
        grid_spec=pltpu.PrefetchScalarGridSpec(
            num_scalar_prefetch=1,
            grid=(1,),
            in_specs=[whole_spec(t.shape) for t in [*flat, *gots]],
            out_specs=[whole_spec((sum(t.shape[0] for t in flat) // 2, columns))]
            + [whole_spec((t.shape[0] // 2, columns)) for t in flat],
        ),
        out_shape=[jax.ShapeDtypeStruct((sum(t.shape[0] for t in flat) // 2, columns), BF)]
        + [jax.ShapeDtypeStruct((t.shape[0] // 2, columns), BF) for t in flat],
        compiler_params=params(),
        cost_estimate=cost(),
        name="sum_sides",
    )(side, *flat, *gots)
    return send, keep


VMEM_LIMIT = 56 * 1024 * 1024


def whole_spec(shape):
    return pl.BlockSpec(shape, lambda *_: (0,) * len(shape))


def dot(left, right):
    return jnp.dot(left, right, preferred_element_type=F32)


def dot_tn(left, right):
    return lax.dot_general(left, right, (((0,), (0,)), ((), ())), preferred_element_type=F32)


def dot_nt(left, right):
    return lax.dot_general(left, right, (((1,), (1,)), ((), ())), preferred_element_type=F32)


def cost(*_):
    return pl.CostEstimate(flops=1, bytes_accessed=1, transcendentals=0)


def params():
    return pltpu.CompilerParams(vmem_limit_bytes=VMEM_LIMIT)


def project_kernel(first, count, me_ref, *refs):
    x_refs, refs = refs[:count], refs[count:]
    wq_ref, wk_ref, wv_ref, cos_ref, sin_ref, scale_ref = refs[:6]
    q_ref, k_ref, v_ref, rq_ref, rk_ref = refs[-5:]
    width = q_ref.shape[0]
    heads = width // HEAD_DIM
    scale = scale_ref[...].reshape(heads, 2, HALF, 1)
    for b in range(count):
        here = slice(b * BLOCK, (b + 1) * BLOCK)
        x = x_refs[b][...]
        at = pl.ds(pl.multiple_of((me_ref[0] ^ (first + b)) * BLOCK, BLOCK), BLOCK)
        cos, sin = cos_ref[:, at][None], sin_ref[:, at][None]
        for w_ref, o_ref, r_ref in ((wq_ref, q_ref, rq_ref), (wk_ref, k_ref, rk_ref)):
            pairs = dot(x, w_ref[...]).T.reshape(heads, 2, HALF, BLOCK)
            one, two = pairs[:, 0], pairs[:, 1]
            ra, rb = one * cos - two * sin, two * cos + one * sin
            square = jnp.sum(ra * ra + rb * rb, axis=1, keepdims=True) * (1.0 / HEAD_DIM)
            r = lax.rsqrt(square + EPSILON)
            r_ref[:, :, here] = r
            out = jnp.stack([ra * r * scale[:, 0], rb * r * scale[:, 1]], axis=1)
            o_ref[:, here] = out.reshape(width, BLOCK).astype(BF)
        v_ref[:, here] = dot(x, wv_ref[...]).T.astype(BF)


def project(me, first, blocks, held, wq, wk, wv, cos, sin, scale):
    count = len(blocks)
    seq = cos.shape[1]
    depth, width = wq.shape
    heads = width // HEAD_DIM
    place = first // count
    tall = pl.BlockSpec((width, count * BLOCK), lambda i, me: (0, place))
    row = pl.BlockSpec((heads, 1, count * BLOCK), lambda i, me: (0, 0, place))
    held = list(held)
    return pl.pallas_call(
        partial(project_kernel, first, count),
        grid_spec=pltpu.PrefetchScalarGridSpec(
            num_scalar_prefetch=1,
            grid=(1,),
            in_specs=[whole_spec((BLOCK, depth))] * count
            + [whole_spec((depth, width))] * 3
            + [whole_spec((HALF, seq))] * 2
            + [whole_spec((width, 1))]
            + [pl.BlockSpec(memory_space=pl.ANY)] * len(held),
            out_specs=[tall, tall, tall, row, row],
        ),
        out_shape=[jax.ShapeDtypeStruct((width, seq), BF)] * 3
        + [jax.ShapeDtypeStruct((heads, 1, seq), F32)] * 2,
        input_output_aliases={count + 7 + i: i for i in range(len(held))},
        compiler_params=params(),
        cost_estimate=cost(6 * count * BLOCK * depth * width, 2 * count * BLOCK * depth + 6 * depth * width),
        name="project",
    )(me, *blocks, wq, wk, wv, cos, sin, scale, *held)


def block_at(me, index):
    return pl.ds(pl.multiple_of((me ^ index) * BLOCK, BLOCK), BLOCK)


def allowed(start, low, first, diagonal):
    key = lax.broadcasted_iota(jnp.int32, (BLOCK, BLOCK), 0)
    seen = key >= start - first
    if diagonal:
        seen = seen & (key <= lax.broadcasted_iota(jnp.int32, (BLOCK, BLOCK), 1))
    return seen


def attend_kernel(me_ref, q_ref, k_ref, v_ref, start_ref, o_ref, l_ref, kn_ref):
    me = me_ref[0]
    width, seq = q_ref.shape
    blocks = seq // BLOCK
    factor = LOG2E / HEAD_DIM**0.5
    for j in range(blocks):
        kn_ref[j * BLOCK : (j + 1) * BLOCK, :] = k_ref[:, block_at(me, j)].T
    for i in range(blocks):
        here = block_at(me, i)
        start = start_ref[:, i * BLOCK : (i + 1) * BLOCK]
        masks = [allowed(start, i, j * BLOCK, i == j) for j in range(i + 1)]
        heads = [slice(h * HEAD_DIM, (h + 1) * HEAD_DIM) for h in range(width // HEAD_DIM)]
        totals = [jnp.zeros((1, BLOCK), F32) for _ in heads]
        outs = [jnp.zeros((HEAD_DIM, BLOCK), F32) for _ in heads]
        for j in range(i + 1):
            scores = [dot(kn_ref[j * BLOCK : (j + 1) * BLOCK, head], q_ref[head, here]) for head in heads]
            probs = [jnp.where(masks[j], jnp.exp2(s * factor), 0.0) for s in scores]
            totals = [t + jnp.sum(p, axis=0, keepdims=True) for t, p in zip(totals, probs)]
            outs = [
                t + dot(v_ref[head, block_at(me, j)], p.astype(BF)) for t, head, p in zip(outs, heads, probs)
            ]
        for h, head in enumerate(heads):
            o_ref[head, here] = (outs[h] * (1.0 / totals[h])).astype(BF)
            l_ref[h, :, here] = jnp.log2(totals[h])


def attend(me, q, k, v, start):
    width, seq = q.shape
    heads = width // HEAD_DIM
    tall = whole_spec((width, seq))
    return pl.pallas_call(
        attend_kernel,
        grid_spec=pltpu.PrefetchScalarGridSpec(
            num_scalar_prefetch=1,
            grid=(1,),
            in_specs=[tall, tall, tall, whole_spec((1, seq))],
            out_specs=[tall, whole_spec((heads, 1, seq))],
            scratch_shapes=[pltpu.VMEM((seq, width), BF)],
        ),
        out_shape=[jax.ShapeDtypeStruct((width, seq), BF), jax.ShapeDtypeStruct((heads, 1, seq), F32)],
        compiler_params=params(),
        cost_estimate=cost(),
        name="attend",
    )(me, q, k, v, start)


PAIR = 2 * HEAD_DIM
GROUP = 2


def attend_back_kernel(
    me_ref, q_ref, k_ref, v_ref, o_ref, do_ref, l_ref, start_ref, rq_ref, rk_ref, cos_ref, sin_ref, scale_ref,
    g_ref, gs_ref, qn_ref, kn_ref, vn_ref, dn_ref, dq_ref, delta_ref,
):
    me = me_ref[0]
    width, seq = q_ref.shape
    blocks = seq // BLOCK
    heads = width // HEAD_DIM
    factor = LOG2E / HEAD_DIM**0.5
    scale = scale_ref[...]

    def rows(j):
        return slice(j * BLOCK, (j + 1) * BLOCK)

    for j in range(blocks):
        here = block_at(me, j)
        qn_ref[rows(j), :] = q_ref[:, here].T
        kn_ref[rows(j), :] = k_ref[:, here].T
        vn_ref[rows(j), :] = v_ref[:, here].T
        dn_ref[rows(j), :] = do_ref[:, here].T
        both = do_ref[:, here].astype(F32) * o_ref[:, here].astype(F32)
        for h in range(heads):
            head = slice(h * HEAD_DIM, (h + 1) * HEAD_DIM)
            delta_ref[h, :, rows(j)] = jnp.sum(both[head], axis=0, keepdims=True)

    def prepare_back(grad, value, r_ref, j, n):
        at = block_at(me, j)
        unit = value.astype(F32) / scale
        grad = grad * (1.0 / HEAD_DIM**0.5)
        gs_ref[...] += jnp.sum(unit * grad, axis=1, keepdims=True)
        g = grad * scale
        cos, sin = cos_ref[:, rows(j)], sin_ref[:, rows(j)]
        out = []
        for h in range(heads):
            head = slice(h * HEAD_DIM, (h + 1) * HEAD_DIM)
            inner = jnp.sum(unit[head] * g[head], axis=0, keepdims=True) * (1.0 / HEAD_DIM)
            part = (g[head] - unit[head] * inner) * r_ref[h, :, at]
            one, two = part[:HALF], part[HALF:]
            out += [one * cos + two * sin, two * cos - one * sin]
        for p in range(width // PAIR):
            pair = jnp.concatenate(out[4 * p : 4 * p + 4], axis=0).T.astype(BF)
            g_ref[at, (3 * p + n) * PAIR : (3 * p + n + 1) * PAIR] = pair

    gs_ref[...] = jnp.zeros_like(gs_ref)
    for j in range(blocks):
        at_j = block_at(me, j)
        masks = [allowed(start_ref[:, rows(i)], i, j * BLOCK, i == j) for i in range(j, blocks)]
        dks = [jnp.zeros((BLOCK, HEAD_DIM), F32) for _ in range(heads)]
        dvs = list(dks)
        for first in range(0, heads, GROUP):
            group = [(h, slice(h * HEAD_DIM, (h + 1) * HEAD_DIM)) for h in range(first, min(first + GROUP, heads))]
            for i in range(j, blocks):
                at_i = block_at(me, i)
                scores = [dot(kn_ref[rows(j), head], q_ref[head, at_i]) for _, head in group]
                dps = [dot(vn_ref[rows(j), head], do_ref[head, at_i]) for _, head in group]
                ps = [
                    jnp.where(masks[i - j], jnp.exp2(s * factor - l_ref[h, :, at_i]), 0.0)
                    for (h, _), s in zip(group, scores)
                ]
                dss = [
                    (p * (dp - delta_ref[h, :, rows(i)])).astype(BF) for (h, _), p, dp in zip(group, ps, dps)
                ]
                for (h, head), p, ds in zip(group, ps, dss):
                    dvs[h] = dvs[h] + dot(p.astype(BF), dn_ref[rows(i), head])
                    dks[h] = dks[h] + dot(ds, qn_ref[rows(i), head])
                    dq = dot(k_ref[head, at_j], ds)
                    if j == 0:
                        dq_ref[head, rows(i)] = dq
                    else:
                        dq_ref[head, rows(i)] += dq
        for p in range(width // PAIR):
            pair = jnp.concatenate(dvs[2 * p : 2 * p + 2], axis=1).astype(BF)
            g_ref[at_j, (3 * p + 2) * PAIR : (3 * p + 3) * PAIR] = pair
        prepare_back(jnp.concatenate(dks, axis=1).T, k_ref[:, at_j], rk_ref, j, 1)
        prepare_back(dq_ref[:, rows(j)], q_ref[:, at_j], rq_ref, j, 0)


def attend_back(me, q, k, v, o, do, l, start, rq, rk, cos, sin, scale):
    width, seq = q.shape
    heads = width // HEAD_DIM
    row = whole_spec((heads, 1, seq))
    return pl.pallas_call(
        attend_back_kernel,
        grid_spec=pltpu.PrefetchScalarGridSpec(
            num_scalar_prefetch=1,
            grid=(1,),
            in_specs=[whole_spec((width, seq))] * 5
            + [row, whole_spec((1, seq)), row, row, whole_spec((HALF, seq)), whole_spec((HALF, seq))]
            + [whole_spec((width, 1))],
            out_specs=[whole_spec((seq, 3 * width)), whole_spec((width, 1))],
            scratch_shapes=[pltpu.VMEM((seq, width), BF)] * 4
            + [pltpu.VMEM((width, seq), F32), pltpu.VMEM((heads, 1, seq), F32)],
        ),
        out_shape=[jax.ShapeDtypeStruct((seq, 3 * width), BF), jax.ShapeDtypeStruct((width, 1), F32)],
        compiler_params=params(),
        cost_estimate=cost(),
        name="attend_back",
    )(me, q, k, v, o, do, l, start, rq, rk, cos, sin, scale)


def root_mean(values):
    return lax.rsqrt(jnp.mean(values * values, axis=-1, keepdims=True) + EPSILON)


def sum_refs(refs):
    total = refs[0][...].astype(F32)
    for ref in refs[1:]:
        total = total + ref[...].astype(F32)
    return total


ROWS = 128


def row_call(kernel, name, blocks, vectors, outs):
    depth = blocks[0].shape[1]
    tile = pl.BlockSpec((ROWS, depth), lambda i: (i, 0))
    return pl.pallas_call(
        kernel,
        grid=(BLOCK // ROWS,),
        in_specs=[tile] * len(blocks) + [whole_spec(t.shape) for t in vectors],
        out_specs=[tile if rows == BLOCK else whole_spec((rows, depth)) for _, rows in outs],
        out_shape=[jax.ShapeDtypeStruct((rows, depth), t) for t, rows in outs],
        compiler_params=params(),
        cost_estimate=cost(),
        name=name,
    )(*blocks, *vectors)


def sum_terms(terms):
    return sum(t.astype(F32) for t in terms)


def middle_update(terms, x, alpha):
    mixed, x = sum_terms(terms), x.astype(F32)
    stepped = x + alpha * (mixed * root_mean(mixed) - x)
    return (stepped * root_mean(stepped)).astype(BF)


def step_back(base, mixed, alpha, grad):
    r_mixed = root_mean(mixed)
    unit = mixed * r_mixed
    apart = unit - base
    stepped = base + alpha * apart
    r = root_mean(stepped)
    value = stepped * r
    grad_step = r * (grad - value * jnp.mean(value * grad, axis=-1, keepdims=True))
    grad_unit = alpha * grad_step
    grad_mixed = r_mixed * (grad_unit - unit * jnp.mean(unit * grad_unit, axis=-1, keepdims=True))
    share = jnp.sum(grad_step * apart, axis=0, keepdims=True)
    return value, grad_step - grad_unit, grad_mixed, share


def add_share(share_ref, share):
    @pl.when(pl.program_id(0) == 0)
    def _():
        share_ref[...] = share

    @pl.when(pl.program_id(0) > 0)
    def _():
        share_ref[...] += share


def last_update(terms, middle, cotangent, alpha):
    n = len(terms)

    def kernel(*refs):
        mid_ref, cot_ref, alpha_ref, out_ref, res_ref, low_ref, share_ref = refs[n:]
        value, res, grad_mixed, share = step_back(
            mid_ref[...].astype(F32), sum_refs(refs[:n]), alpha_ref[...], cot_ref[...].astype(F32)
        )
        out_ref[...] = value.astype(BF)
        res_ref[...] = res.astype(BF)
        low_ref[...] = grad_mixed.astype(BF)
        add_share(share_ref, share)

    return row_call(kernel, "last_update", [*terms, middle, cotangent], [alpha], [(BF, BLOCK), (BF, BLOCK), (BF, BLOCK), (F32, 1)])


def joint_sums(ends, width):
    rows, extra = ends[0][0].shape[0], ends[0][1].shape[0]

    def kernel(*refs):
        ins, outs = refs[: 3 * len(ends)], refs[3 * len(ends) :]
        for i in range(len(ends)):
            held_ref, small_ref, got_ref = ins[3 * i : 3 * i + 3]
            total = held_ref[...].astype(F32) + got_ref[:rows, :].astype(F32)
            for n, out_ref in enumerate(outs[:3]):
                out_ref[:, i * PAIR : (i + 1) * PAIR] = total[:, n * PAIR : (n + 1) * PAIR]
            outs[3][i * PAIR : (i + 1) * PAIR, :] = total[:, 3 * PAIR :].T
        outs[4][...] = small_ref[...].astype(F32) + got_ref[rows:, :].astype(F32)

    return pl.pallas_call(
        kernel,
        out_shape=[jax.ShapeDtypeStruct((rows, width), F32)] * 3
        + [jax.ShapeDtypeStruct((width, rows), F32), jax.ShapeDtypeStruct((extra, 4 * PAIR), F32)],
        compiler_params=params(),
        cost_estimate=cost(),
        name="joint_sums",
    )(*[t for end in ends for t in end])


def input_update(terms, grad, hint):
    n = len(terms)

    def kernel(*refs):
        grad_ref, hint_ref, out_ref = refs[n:]
        out_ref[...] = sum_refs(refs[:n]) + grad_ref[...].astype(F32)

    return row_call(kernel, "input_update", [*terms, grad], [hint], [(F32, BLOCK)])[0]


def middle_back(terms, x, grads, grad_res, alpha):
    grad = sum_terms([*grads, grad_res])
    _, res, grad_mixed, share = step_back(x.astype(F32), sum_terms(terms), alpha, grad)
    return res.astype(BF), grad_mixed.astype(BF), share


def body(
    n_mp, x_bits, z_bits,
    hidden_in, doc_index, doc_position, w_query, w_key, w_value, w_out, w_up, w_gate, w_down,
    score_scale, up_scale, gate_scale, alpha_attention, alpha_feedforward, cotangent,
):
    depth, width = w_query.shape
    seq = doc_position.shape[0]
    me = lax.axis_index("mp").astype(jnp.int32).reshape(1)
    place = lax.axis_index("dp").astype(jnp.int32)
    x_first = x_bits + z_bits
    z_first = z_bits[:1] + x_bits + z_bits[1:]
    n_dp = 1 << len(x_first)

    tokens = jnp.arange(seq, dtype=jnp.int32)
    start = (tokens - doc_position).reshape(1, seq)
    steps = jnp.arange(HALF).astype(F32)
    inverse = jnp.exp(steps * (-2.0 * jnp.log(10000.0) / HEAD_DIM))
    angles = inverse[:, None] * doc_position.astype(F32)[None, :]
    cos, sin = jnp.cos(angles), jnp.sin(angles)
    scale = score_scale.reshape(width, 1)
    alpha_attention = alpha_attention.reshape(1, depth)
    alpha_feedforward = alpha_feedforward.reshape(1, depth)
    up_scale, gate_scale = up_scale.reshape(1, -1), gate_scale.reshape(1, -1)
    far_count = n_mp - 2

    def join(blocks):
        return jnp.concatenate(blocks, axis=0)

    def cut(parts):
        return [parts[b * BLOCK : (b + 1) * BLOCK] for b in range(parts.shape[0] // BLOCK)]

    near = slice(0, 2 * BLOCK)
    rest = slice(2 * BLOCK, None)
    pairs = range(width // PAIR)

    def columns(w, i):
        return w[:, i * PAIR : (i + 1) * PAIR]

    w_joint = jnp.concatenate(
        [columns(w, i) for i in pairs for w in (w_query, w_key, w_value)], axis=1
    )

    coming = gather_start(hidden_in, n_mp)
    x_near = [hidden_in, swap(hidden_in, 1, n_mp)]
    held = project(me, 0, x_near, [], w_query, w_key, w_value, cos, sin, scale)
    x_far = gather_finish(coming, held[0], n_mp)
    for i in range(0, far_count, 2):
        held = project(me, 2 + i, x_far[i : i + 2], held, w_query, w_key, w_value, cos, sin, scale)
    q, k, v, rq, rk = held
    o, l = attend(me, q, k, v, start)
    far_terms, sent = scatter_far(cut(dot_tn(o[:, rest], w_out).astype(BF)), n_mp)
    parts = cut(dot_tn(after(o, sent)[:, near], w_out).astype(BF))
    attn_terms = [parts[0], swap(parts[1], 1, n_mp), *far_terms]
    middle_low = middle_update(attn_terms, hidden_in, alpha_attention)

    def unit(rows):
        u = dot(rows, w_up)
        g = dot(rows, w_gate)
        gate = g * gate_scale
        inner = (u * up_scale * (gate / (1.0 + jnp.exp(-gate)))).astype(BF)
        return u.astype(BF), g.astype(BF), inner, dot(inner, w_down).astype(BF)

    coming = gather_start(middle_low, n_mp)
    mid_near = join([middle_low, swap(middle_low, 1, n_mp)])
    u0, g0, inner0, parts = unit(mid_near)
    mid_far = join(gather_finish(coming, parts, n_mp))
    u1, g1, inner1, far = unit(mid_far)
    far_terms, sent = scatter_far(cut(far), n_mp)
    parts = cut(after(parts, sent))
    x_all = jnp.concatenate([*x_near, *x_far[:-1], after(x_far[-1], sent)], axis=0)
    ff_terms = [parts[0], swap(parts[1], 1, n_mp), *far_terms]
    ff_terms[-1], x_all = lax.optimization_barrier((ff_terms[-1], x_all))
    layer_out, grad_res, grad_low, share_ff = last_update(ff_terms, middle_low, cotangent, alpha_feedforward)

    def unit_back(rows, u, g):
        grad = dot_nt(rows, w_down)
        u, g = u.astype(F32), g.astype(F32)
        gate = g * gate_scale
        sig = 1.0 / (1.0 + jnp.exp(-gate))
        by_up = grad * (gate * sig)
        by_gate = grad * (u * up_scale) * (sig * (1.0 + gate * (1.0 - sig)))
        du, dg = (by_up * up_scale).astype(BF), (by_gate * gate_scale).astype(BF)
        shares = jnp.stack([jnp.sum(by_up * u, axis=0), jnp.sum(by_gate * g, axis=0)])
        return du, dg, shares

    def unit_parts(du, dg):
        return (dot_nt(du, w_up) + dot_nt(dg, w_gate)).astype(BF)

    order = Order()
    coming = gather_start(grad_low, n_mp)
    g_near = [grad_low, order.fill(grad_low, swap(grad_low, 1, n_mp))]
    g_near = join(g_near)
    du0, dg0, shares0 = unit_back(g_near, u0, g0)
    near_parts = order.mark(unit_parts(du0, dg0))
    g_far = gather_finish(coming, near_parts, n_mp)
    g_far = join(g_far)
    grad_down = Reduction(order, [(dot_tn(g_near, inner0) + dot_tn(g_far, inner1)).astype(BF)], x_first, place)
    du1, dg1, shares1 = unit_back(order.tie(g_far), u1, g1)
    far = unit_parts(du1, dg1)
    far_terms, sent = scatter_far(cut(far), n_mp, order)
    order.mark(sent)
    unit_scales = shares0 + shares1

    def over_tokens(near, far):
        return (dot_tn(mid_near, near) + dot_tn(mid_far, order.tie(far))).astype(BF)

    grad_gate = Reduction(order, [over_tokens(dg0, dg1)], z_first, place)
    grad_up = Reduction(order, [over_tokens(du0, du1)], x_first, place)
    parts = cut(order.tie(near_parts))
    mid_terms = [parts[0], swap(parts[1], 1, n_mp), *far_terms]
    mid_terms[-1] = order.fill(sent, order.tie(mid_terms[-1]))
    grad_x, grad_low, share_attn = middle_back(attn_terms, hidden_in, mid_terms, grad_res, alpha_attention)
    order.mark(grad_low)

    coming = gather_start(grad_low, n_mp)
    a_near = [grad_low, swap(grad_low, 1, n_mp)]
    do_near = order.mark(dot_nt(w_out, order.tie(join(a_near))).astype(BF))
    grad_down.step()
    grad_gate.step()
    a_far = gather_finish(coming, order.last, n_mp, order, grad_low)
    do = order.mark(jnp.concatenate([do_near, dot_nt(w_out, join(a_far)).astype(BF)], axis=1))
    a_all = join(a_near + a_far)
    grad_up.step()

    def rows_first(grad):
        return with_layout_constraint(grad.astype(BF), Layout(major_to_minor=(0, 1)))

    grad_joint, grad_scale = attend_back(me, q, k, v, o, order.tie(do), l, start, rq, rk, cos, sin, scale)
    order.mark(grad_joint)
    grad_out = lax.dot_general(a_all, order.tie(o), (((0,), (1,)), ((), ())), preferred_element_type=F32)
    grad_out = rows_first(grad_out)
    shares = jnp.concatenate([share_attn, share_ff], axis=0).reshape(2 * n_mp, n_dp, -1)
    early = [shares.transpose(1, 0, 2), unit_scales.reshape(2, n_dp, -1).transpose(1, 0, 2)]
    joints = []
    for i in pairs:
        grads = rows_first(dot_tn(order.tie(x_all), grad_joint[:, 3 * i * PAIR : 3 * (i + 1) * PAIR]))
        grads = jnp.concatenate([grads, columns(grad_out, i)], axis=1)
        small = early if i == 0 else []
        if i == pairs[-1]:
            small = small + [grad_scale.reshape(1, n_dp, -1).transpose(1, 0, 2)]
        small = jnp.concatenate([t.reshape(n_dp, 1, -1) for t in small], axis=2).astype(BF)
        small = jnp.pad(small, ((0, 0), (0, 15), (0, 4 * PAIR - small.shape[2]))).reshape(-1, 4 * PAIR)
        joints.append(Reduction(order, [grads, small], x_first if i % 2 else z_first, place))
    while len(grad_up.bits) > 1:
        for reduction in (grad_up, grad_gate, grad_down):
            reduction.step()
    grad_up.merge([grad_gate, grad_down])
    far = dot_nt(order.tie(grad_joint)[rest], w_joint).astype(BF)
    far_terms, sent = scatter_far(cut(far), n_mp, order)
    order.mark(sent)
    joints[-1].step()
    parts = cut(dot_nt(order.tie(grad_joint)[near], w_joint).astype(BF))
    order.mark(parts[1])
    in_terms = [parts[0], swap(parts[1], 1, n_mp), *far_terms]
    for reduction in joints:
        while len(reduction.bits) > 1:
            reduction.step()
    in_terms[-1] = order.fill(sent, order.tie(in_terms[-1]))
    grad_input = input_update(in_terms, grad_x, order.hint)
    order.mark(grad_input)
    for reduction in joints:
        reduction.step()
    order.mark(grad_input)
    grad_up, grad_gate, grad_down = [h.astype(F32) + g.astype(F32) for h, g in grad_up.finish()]
    order.mark(grad_input)
    while joints[0].bits:
        for reduction in joints:
            reduction.step()
    ends = [order.tie(*reduction.held, reduction.got) for reduction in joints]
    small = [ends[0][1][0].astype(F32) + ends[0][2][depth // n_dp].astype(F32)]
    shares = small[0][: 2 * n_mp * (depth // n_mp // n_dp)].reshape(2, n_mp, -1)
    shares = [lax.dynamic_index_in_dim(shares, me[0] ^ b, 1, keepdims=False).astype(BF) for b in range(n_mp)]
    alpha = shares[0].astype(F32)
    pieces = {b: t for b, t in enumerate(shares) if b}
    bit = n_mp // 2
    while bit:
        for b in [b for b in list(pieces) if b & bit and b != bit]:
            pieces[b ^ bit] = add_low(pieces[b ^ bit], swap(pieces.pop(b), bit, n_mp))
        alpha = alpha + swap(pieces.pop(bit), bit, n_mp).astype(F32)
        bit //= 2
    scale_rows = small[0][shares[0].shape[1] * 2 * n_mp :]
    count = w_up.shape[1] // n_dp
    up_share, gate_share, score = scale_rows[:count], scale_rows[count : 2 * count], scale_rows[2 * count :]
    alpha_a, alpha_f = alpha[0], alpha[1]
    grad_query, grad_key, grad_value, grad_out, last = joint_sums(ends, width)
    score = (score if len(joints) == 1 else last[0])[: width // n_dp]
    grad_down = grad_down.T
    return (
        layer_out,
        grad_input,
        grad_query,
        grad_key,
        grad_value,
        grad_out,
        grad_up,
        grad_gate,
        grad_down,
        score,
        up_share,
        gate_share,
        alpha_a,
        alpha_f,
    )


def solution(mesh):
    n_dp, n_mp = mesh.shape["dp"], mesh.shape["mp"]
    bits = [1 << i for i in range(n_dp.bit_length() - 1)]
    cut = len(bits) // 2
    token = P(("dp", "mp"), None)
    split = P(("mp", "dp"))
    return jax.shard_map(
        partial(body, n_mp, bits[:cut], bits[cut:]),
        mesh=mesh,
        in_specs=(
            token, P("dp"), P("dp"), P(None, "mp"), P(None, "mp"), P(None, "mp"), P("mp", None),
            P(None, "mp"), P(None, "mp"), P("mp", None), P("mp"), P("mp"), P("mp"), P(), P(), token,
        ),
        out_specs=(
            token, token, P("dp", "mp"), P("dp", "mp"), P("dp", "mp"), P("mp", "dp"),
            P("dp", "mp"), P("dp", "mp"), P("mp", "dp"), split, split, split, split, split,
        ),
        check_vma=False,
    )
```

```python
from functools import partial

import jax
import jax.numpy as jnp
from jax import lax
from jax.experimental import pallas as pl
from jax.experimental.layout import Layout, with_layout_constraint
from jax.experimental.pallas import tpu as pltpu
from jax.sharding import PartitionSpec as P

HEAD_DIM = 64
HALF = HEAD_DIM // 2
BLOCK = 256
EPSILON = 1e-06
LOG2E = 1.4426950408889634
FILL = 20_000_000_000
BF = jnp.bfloat16
F32 = jnp.float32


def swap(value, bit, size, name="mp"):
    return lax.ppermute(value, name, [(i, i ^ bit) for i in range(size)])


def gather_start(own, size):
    blocks = {0: own}
    bit = size // 2
    while bit > 1:
        blocks.update({b ^ bit: swap(v, bit, size) for b, v in list(blocks.items())})
        bit //= 2
    return {b: v for b, v in blocks.items() if b}


def gather_finish(blocks, done, size, order=None, own=None):
    blocks = {b: after(v, done) for b, v in blocks.items()}
    if order is not None:
        blocks = {b: order.fill(own, v) for b, v in blocks.items()}
    for b, v in list(blocks.items()):
        got = swap(v, 1, size)
        blocks[b ^ 1] = got if order is None else order.fill(v, got)
    return [blocks[b] for b in range(2, size)]


def add_low(left, right):
    return (left.astype(F32) + right.astype(F32)).astype(BF)


def scatter_far(far, size, order=None):
    sums = {}
    for b in range(size - 2, 1, -2):
        got = swap(far[b - 1], 1, size)
        if order is not None:
            got = order.fill(far[b - 1], got)
        sums[b] = add_low(far[b - 2], got)
    terms = []
    bit = 2
    while bit < size:
        kept = {}
        for b in sorted(sums, reverse=True):
            if not b & bit:
                kept[b] = add_low(sums[b], swap(sums[b ^ bit], bit, size))
            elif b == bit:
                sent = sums[b]
                terms.append(swap(sent, bit, size))
        sums = kept
        bit *= 2
    return terms, sent


def after(value, done):
    return lax.optimization_barrier((value, done))[0]


def stand_in_kernel(mark_ref, sent_ref, out_ref):
    pass


class Order:
    def __init__(self):
        self.last = None
        self.hint = jnp.zeros((8, 128), F32)

    def fill(self, sent, *got):
        hint = pl.pallas_call(
            stand_in_kernel,
            in_specs=[pl.BlockSpec(memory_space=pl.ANY)] * 2,
            out_specs=pl.BlockSpec(memory_space=pl.ANY),
            out_shape=jax.ShapeDtypeStruct((8, 128), F32),
            input_output_aliases={0: 0},
            cost_estimate=pl.CostEstimate(flops=FILL, bytes_accessed=0, transcendentals=0),
            name="stand_in",
        )(self.hint, sent)
        *got, self.hint = lax.optimization_barrier((*got, hint))
        return got if len(got) > 1 else got[0]

    def tie(self, *values):
        if self.last is not None:
            values = lax.optimization_barrier((*values, self.last))[:-1]
        return values if len(values) > 1 else values[0]

    def mark(self, value):
        self.last = value
        return value


def take(rows, place, bits, left, other):
    at = (place // bits[0]) % 2
    lead = 1 << left.index(bits[0])
    split = rows.reshape(lead, 2, rows.shape[0] // (2 * lead), rows.shape[1])
    half = lax.dynamic_slice_in_dim(split, 1 - at if other else at, 1, 1)
    return half.reshape(rows.shape[0] // 2, rows.shape[1])


class Reduction:
    def __init__(self, order, grads, bits, place):
        self.order, self.bits, self.place = order, list(bits), place
        self.size = 1 << len(bits)
        self.left = [1 << i for i in reversed(range(len(bits)))]
        self.send([[t] for t in grads])

    def send(self, sums):
        sides = [[take(t, self.place, self.bits, self.left, other) for (t,) in sums] for other in (True, False)]
        part = sides[0][0] if len(sums) == 1 else jnp.concatenate(sides[0], axis=0)
        self.swap(part, sides[1])

    def swap(self, part, held):
        self.held = list(held)
        self.got = swap(self.order.mark(part), self.bits[0], self.size, "dp")
        self.left.remove(self.bits.pop(0))

    def arrived(self):
        *held, got = self.order.tie(*self.held, self.got)
        sums, row = [], 0
        for t in held:
            sums.append([t, got[row : row + t.shape[0]]])
            row += t.shape[0]
        return sums

    def merge(self, others):
        held, gots = [], []
        for reduction in [self, *others]:
            *more, got = self.order.tie(*reduction.held, reduction.got)
            held.append(more)
            gots.append(got)
        bit = self.bits[0]
        side = (self.place // bit) % 2
        self.swap(*sum_sides(held, gots, side.reshape(1), 1 << self.left.index(bit)))

    def step(self):
        self.merge([])

    def finish(self):
        while self.bits:
            self.step()
        return self.arrived()


def sum_sides(held, gots, side, lead):
    flat = [t for group in held for t in group]
    columns = flat[0].shape[1]

    def kernel(side_ref, *refs):
        held_refs, refs = refs[: len(flat)], refs[len(flat) :]
        got_refs, (send_ref, *keep_refs) = refs[: len(gots)], refs[len(gots) :]
        own = side_ref[0]
        row = k = 0
        for group, got_ref in zip(held, got_refs):
            base = 0
            for t in group:
                step = t.shape[0] // (2 * lead)
                for n in range(lead):
                    for out_ref, out_row, at in (
                        (send_ref, row, 2 * n + 1 - own),
                        (keep_refs[k], n * step, 2 * n + own),
                    ):
                        at = pl.multiple_of(at * step, 16)
                        total = held_refs[k][pl.ds(at, step), :].astype(F32)
                        total = total + got_ref[pl.ds(pl.multiple_of(base + at, 16), step), :].astype(F32)
                        out_ref[out_row : out_row + step, :] = total.astype(BF)
                    row += step
                base += t.shape[0]
                k += 1

    send, *keep = pl.pallas_call(
        kernel,
        grid_spec=pltpu.PrefetchScalarGridSpec(
            num_scalar_prefetch=1,
            grid=(1,),
            in_specs=[whole_spec(t.shape) for t in [*flat, *gots]],
            out_specs=[whole_spec((sum(t.shape[0] for t in flat) // 2, columns))]
            + [whole_spec((t.shape[0] // 2, columns)) for t in flat],
        ),
        out_shape=[jax.ShapeDtypeStruct((sum(t.shape[0] for t in flat) // 2, columns), BF)]
        + [jax.ShapeDtypeStruct((t.shape[0] // 2, columns), BF) for t in flat],
        compiler_params=params(),
        cost_estimate=cost(),
        name="sum_sides",
    )(side, *flat, *gots)
    return send, keep


VMEM_LIMIT = 24 * 1024 * 1024


def whole_spec(shape):
    return pl.BlockSpec(shape, lambda *_: (0,) * len(shape))


def dot(left, right):
    return jnp.dot(left, right, preferred_element_type=F32)


def dot_tn(left, right):
    return lax.dot_general(left, right, (((0,), (0,)), ((), ())), preferred_element_type=F32)


def dot_nt(left, right):
    return lax.dot_general(left, right, (((1,), (1,)), ((), ())), preferred_element_type=F32)


def cost(*_):
    return pl.CostEstimate(flops=1, bytes_accessed=1, transcendentals=0)


def params():
    return pltpu.CompilerParams(vmem_limit_bytes=VMEM_LIMIT)


def project_kernel(first, count, me_ref, *refs):
    x_refs, refs = refs[:count], refs[count:]
    wq_ref, wk_ref, wv_ref, cos_ref, sin_ref, scale_ref = refs[:6]
    q_ref, k_ref, v_ref, rq_ref, rk_ref = refs[-5:]
    width = q_ref.shape[0]
    heads = width // HEAD_DIM
    scale = scale_ref[...].reshape(heads, 2, HALF, 1)
    for b in range(count):
        here = slice(b * BLOCK, (b + 1) * BLOCK)
        x = x_refs[b][...]
        at = pl.ds(pl.multiple_of((me_ref[0] ^ (first + b)) * BLOCK, BLOCK), BLOCK)
        cos, sin = cos_ref[:, at][None], sin_ref[:, at][None]
        for w_ref, o_ref, r_ref in ((wq_ref, q_ref, rq_ref), (wk_ref, k_ref, rk_ref)):
            pairs = dot(x, w_ref[...]).T.reshape(heads, 2, HALF, BLOCK)
            one, two = pairs[:, 0], pairs[:, 1]
            ra, rb = one * cos - two * sin, two * cos + one * sin
            square = jnp.sum(ra * ra + rb * rb, axis=1, keepdims=True) * (1.0 / HEAD_DIM)
            r = lax.rsqrt(square + EPSILON)
            r_ref[:, :, here] = r
            out = jnp.stack([ra * r * scale[:, 0], rb * r * scale[:, 1]], axis=1)
            o_ref[:, here] = out.reshape(width, BLOCK).astype(BF)
        v_ref[:, here] = dot(x, wv_ref[...]).T.astype(BF)


def project(me, first, blocks, held, wq, wk, wv, cos, sin, scale):
    count = len(blocks)
    seq = cos.shape[1]
    depth, width = wq.shape
    heads = width // HEAD_DIM
    place = first // count
    tall = pl.BlockSpec((width, count * BLOCK), lambda i, me: (0, place))
    row = pl.BlockSpec((heads, 1, count * BLOCK), lambda i, me: (0, 0, place))
    held = list(held)
    return pl.pallas_call(
        partial(project_kernel, first, count),
        grid_spec=pltpu.PrefetchScalarGridSpec(
            num_scalar_prefetch=1,
            grid=(1,),
            in_specs=[whole_spec((BLOCK, depth))] * count
            + [whole_spec((depth, width))] * 3
            + [whole_spec((HALF, seq))] * 2
            + [whole_spec((width, 1))]
            + [pl.BlockSpec(memory_space=pl.ANY)] * len(held),
            out_specs=[tall, tall, tall, row, row],
        ),
        out_shape=[jax.ShapeDtypeStruct((width, seq), BF)] * 3
        + [jax.ShapeDtypeStruct((heads, 1, seq), F32)] * 2,
        input_output_aliases={count + 7 + i: i for i in range(len(held))},
        compiler_params=params(),
        cost_estimate=cost(6 * count * BLOCK * depth * width, 2 * count * BLOCK * depth + 6 * depth * width),
        name="project",
    )(me, *blocks, wq, wk, wv, cos, sin, scale, *held)


def block_at(me, index):
    return pl.ds(pl.multiple_of((me ^ index) * BLOCK, BLOCK), BLOCK)


def allowed(start, low, first, diagonal):
    key = lax.broadcasted_iota(jnp.int32, (BLOCK, BLOCK), 0)
    seen = key >= start - first
    if diagonal:
        seen = seen & (key <= lax.broadcasted_iota(jnp.int32, (BLOCK, BLOCK), 1))
    return seen


def attend_kernel(me_ref, q_ref, k_ref, v_ref, start_ref, o_ref, l_ref, kn_ref):
    me = me_ref[0]
    width, seq = q_ref.shape
    blocks = seq // BLOCK
    factor = LOG2E / HEAD_DIM**0.5
    for j in range(blocks):
        kn_ref[j * BLOCK : (j + 1) * BLOCK, :] = k_ref[:, block_at(me, j)].T
    for i in range(blocks):
        here = block_at(me, i)
        start = start_ref[:, i * BLOCK : (i + 1) * BLOCK]
        masks = [allowed(start, i, j * BLOCK, i == j) for j in range(i + 1)]
        heads = [slice(h * HEAD_DIM, (h + 1) * HEAD_DIM) for h in range(width // HEAD_DIM)]
        totals = [jnp.zeros((1, BLOCK), F32) for _ in heads]
        outs = [jnp.zeros((HEAD_DIM, BLOCK), F32) for _ in heads]
        for j in range(i + 1):
            scores = [dot(kn_ref[j * BLOCK : (j + 1) * BLOCK, head], q_ref[head, here]) for head in heads]
            probs = [jnp.where(masks[j], jnp.exp2(s * factor), 0.0) for s in scores]
            totals = [t + jnp.sum(p, axis=0, keepdims=True) for t, p in zip(totals, probs)]
            outs = [
                t + dot(v_ref[head, block_at(me, j)], p.astype(BF)) for t, head, p in zip(outs, heads, probs)
            ]
        for h, head in enumerate(heads):
            o_ref[head, here] = (outs[h] * (1.0 / totals[h])).astype(BF)
            l_ref[h, :, here] = jnp.log2(totals[h])


def attend(me, q, k, v, start):
    width, seq = q.shape
    heads = width // HEAD_DIM
    tall = whole_spec((width, seq))
    return pl.pallas_call(
        attend_kernel,
        grid_spec=pltpu.PrefetchScalarGridSpec(
            num_scalar_prefetch=1,
            grid=(1,),
            in_specs=[tall, tall, tall, whole_spec((1, seq))],
            out_specs=[tall, whole_spec((heads, 1, seq))],
            scratch_shapes=[pltpu.VMEM((seq, width), BF)],
        ),
        out_shape=[jax.ShapeDtypeStruct((width, seq), BF), jax.ShapeDtypeStruct((heads, 1, seq), F32)],
        compiler_params=params(),
        cost_estimate=cost(),
        name="attend",
    )(me, q, k, v, start)


PAIR = 2 * HEAD_DIM
GROUP = 2


def attend_back_kernel(
    me_ref, q_ref, k_ref, v_ref, o_ref, do_ref, l_ref, start_ref, rq_ref, rk_ref, cos_ref, sin_ref, scale_ref,
    g_ref, gs_ref, qn_ref, kn_ref, vn_ref, dn_ref, dq_ref, delta_ref,
):
    me = me_ref[0]
    width, seq = q_ref.shape
    blocks = seq // BLOCK
    heads = width // HEAD_DIM
    factor = LOG2E / HEAD_DIM**0.5
    scale = scale_ref[...]

    def rows(j):
        return slice(j * BLOCK, (j + 1) * BLOCK)

    for j in range(blocks):
        here = block_at(me, j)
        qn_ref[rows(j), :] = q_ref[:, here].T
        kn_ref[rows(j), :] = k_ref[:, here].T
        vn_ref[rows(j), :] = v_ref[:, here].T
        dn_ref[rows(j), :] = do_ref[:, here].T
        both = do_ref[:, here].astype(F32) * o_ref[:, here].astype(F32)
        for h in range(heads):
            head = slice(h * HEAD_DIM, (h + 1) * HEAD_DIM)
            delta_ref[h, :, rows(j)] = jnp.sum(both[head], axis=0, keepdims=True)

    def prepare_back(grad, value, r_ref, j, n):
        at = block_at(me, j)
        unit = value.astype(F32) / scale
        grad = grad * (1.0 / HEAD_DIM**0.5)
        gs_ref[...] += jnp.sum(unit * grad, axis=1, keepdims=True)
        g = grad * scale
        cos, sin = cos_ref[:, rows(j)], sin_ref[:, rows(j)]
        out = []
        for h in range(heads):
            head = slice(h * HEAD_DIM, (h + 1) * HEAD_DIM)
            inner = jnp.sum(unit[head] * g[head], axis=0, keepdims=True) * (1.0 / HEAD_DIM)
            part = (g[head] - unit[head] * inner) * r_ref[h, :, at]
            one, two = part[:HALF], part[HALF:]
            out += [one * cos + two * sin, two * cos - one * sin]
        for p in range(width // PAIR):
            pair = jnp.concatenate(out[4 * p : 4 * p + 4], axis=0).T.astype(BF)
            g_ref[at, (3 * p + n) * PAIR : (3 * p + n + 1) * PAIR] = pair

    gs_ref[...] = jnp.zeros_like(gs_ref)
    for j in range(blocks):
        at_j = block_at(me, j)
        masks = [allowed(start_ref[:, rows(i)], i, j * BLOCK, i == j) for i in range(j, blocks)]
        dks = [jnp.zeros((BLOCK, HEAD_DIM), F32) for _ in range(heads)]
        dvs = list(dks)
        for first in range(0, heads, GROUP):
            group = [(h, slice(h * HEAD_DIM, (h + 1) * HEAD_DIM)) for h in range(first, min(first + GROUP, heads))]
            for i in range(j, blocks):
                at_i = block_at(me, i)
                scores = [dot(kn_ref[rows(j), head], q_ref[head, at_i]) for _, head in group]
                dps = [dot(vn_ref[rows(j), head], do_ref[head, at_i]) for _, head in group]
                ps = [
                    jnp.where(masks[i - j], jnp.exp2(s * factor - l_ref[h, :, at_i]), 0.0)
                    for (h, _), s in zip(group, scores)
                ]
                dss = [
                    (p * (dp - delta_ref[h, :, rows(i)])).astype(BF) for (h, _), p, dp in zip(group, ps, dps)
                ]
                for (h, head), p, ds in zip(group, ps, dss):
                    dvs[h] = dvs[h] + dot(p.astype(BF), dn_ref[rows(i), head])
                    dks[h] = dks[h] + dot(ds, qn_ref[rows(i), head])
                    dq = dot(k_ref[head, at_j], ds)
                    if j == 0:
                        dq_ref[head, rows(i)] = dq
                    else:
                        dq_ref[head, rows(i)] += dq
        for p in range(width // PAIR):
            pair = jnp.concatenate(dvs[2 * p : 2 * p + 2], axis=1).astype(BF)
            g_ref[at_j, (3 * p + 2) * PAIR : (3 * p + 3) * PAIR] = pair
        prepare_back(jnp.concatenate(dks, axis=1).T, k_ref[:, at_j], rk_ref, j, 1)
        prepare_back(dq_ref[:, rows(j)], q_ref[:, at_j], rq_ref, j, 0)


def attend_back(me, q, k, v, o, do, l, start, rq, rk, cos, sin, scale):
    width, seq = q.shape
    heads = width // HEAD_DIM
    row = whole_spec((heads, 1, seq))
    return pl.pallas_call(
        attend_back_kernel,
        grid_spec=pltpu.PrefetchScalarGridSpec(
            num_scalar_prefetch=1,
            grid=(1,),
            in_specs=[whole_spec((width, seq))] * 5
            + [row, whole_spec((1, seq)), row, row, whole_spec((HALF, seq)), whole_spec((HALF, seq))]
            + [whole_spec((width, 1))],
            out_specs=[whole_spec((seq, 3 * width)), whole_spec((width, 1))],
            scratch_shapes=[pltpu.VMEM((seq, width), BF)] * 4
            + [pltpu.VMEM((width, seq), F32), pltpu.VMEM((heads, 1, seq), F32)],
        ),
        out_shape=[jax.ShapeDtypeStruct((seq, 3 * width), BF), jax.ShapeDtypeStruct((width, 1), F32)],
        compiler_params=params(),
        cost_estimate=cost(),
        name="attend_back",
    )(me, q, k, v, o, do, l, start, rq, rk, cos, sin, scale)


def root_mean(values):
    return lax.rsqrt(jnp.mean(values * values, axis=-1, keepdims=True) + EPSILON)


def sum_refs(refs):
    total = refs[0][...].astype(F32)
    for ref in refs[1:]:
        total = total + ref[...].astype(F32)
    return total


ROWS = 128


def row_call(kernel, name, blocks, vectors, outs):
    depth = blocks[0].shape[1]
    tile = pl.BlockSpec((ROWS, depth), lambda i: (i, 0))
    return pl.pallas_call(
        kernel,
        grid=(BLOCK // ROWS,),
        in_specs=[tile] * len(blocks) + [whole_spec(t.shape) for t in vectors],
        out_specs=[tile if rows == BLOCK else whole_spec((rows, depth)) for _, rows in outs],
        out_shape=[jax.ShapeDtypeStruct((rows, depth), t) for t, rows in outs],
        compiler_params=params(),
        cost_estimate=cost(),
        name=name,
    )(*blocks, *vectors)


def sum_terms(terms):
    return sum(t.astype(F32) for t in terms)


def middle_update(terms, x, alpha):
    mixed, x = sum_terms(terms), x.astype(F32)
    stepped = x + alpha * (mixed * root_mean(mixed) - x)
    return (stepped * root_mean(stepped)).astype(BF)


def step_back(base, mixed, alpha, grad):
    r_mixed = root_mean(mixed)
    unit = mixed * r_mixed
    apart = unit - base
    stepped = base + alpha * apart
    r = root_mean(stepped)
    value = stepped * r
    grad_step = r * (grad - value * jnp.mean(value * grad, axis=-1, keepdims=True))
    grad_unit = alpha * grad_step
    grad_mixed = r_mixed * (grad_unit - unit * jnp.mean(unit * grad_unit, axis=-1, keepdims=True))
    share = jnp.sum(grad_step * apart, axis=0, keepdims=True)
    return value, grad_step - grad_unit, grad_mixed, share


def add_share(share_ref, share):
    @pl.when(pl.program_id(0) == 0)
    def _():
        share_ref[...] = share

    @pl.when(pl.program_id(0) > 0)
    def _():
        share_ref[...] += share


def last_update(terms, middle, cotangent, alpha):
    n = len(terms)

    def kernel(*refs):
        mid_ref, cot_ref, alpha_ref, out_ref, res_ref, low_ref, share_ref = refs[n:]
        value, res, grad_mixed, share = step_back(
            mid_ref[...].astype(F32), sum_refs(refs[:n]), alpha_ref[...], cot_ref[...].astype(F32)
        )
        out_ref[...] = value.astype(BF)
        res_ref[...] = res.astype(BF)
        low_ref[...] = grad_mixed.astype(BF)
        add_share(share_ref, share)

    return row_call(kernel, "last_update", [*terms, middle, cotangent], [alpha], [(BF, BLOCK), (BF, BLOCK), (BF, BLOCK), (F32, 1)])


def joint_sums(ends, width):
    rows, extra = ends[0][0].shape[0], ends[0][1].shape[0]

    def kernel(*refs):
        ins, outs = refs[: 3 * len(ends)], refs[3 * len(ends) :]
        for i in range(len(ends)):
            held_ref, small_ref, got_ref = ins[3 * i : 3 * i + 3]
            total = held_ref[...].astype(F32) + got_ref[:rows, :].astype(F32)
            for n, out_ref in enumerate(outs[:3]):
                out_ref[:, i * PAIR : (i + 1) * PAIR] = total[:, n * PAIR : (n + 1) * PAIR]
            outs[3][i * PAIR : (i + 1) * PAIR, :] = total[:, 3 * PAIR :].T
        outs[4][...] = small_ref[...].astype(F32) + got_ref[rows:, :].astype(F32)

    return pl.pallas_call(
        kernel,
        out_shape=[jax.ShapeDtypeStruct((rows, width), F32)] * 3
        + [jax.ShapeDtypeStruct((width, rows), F32), jax.ShapeDtypeStruct((extra, 4 * PAIR), F32)],
        compiler_params=params(),
        cost_estimate=cost(),
        name="joint_sums",
    )(*[t for end in ends for t in end])


def input_update(terms, grad, hint):
    n = len(terms)

    def kernel(*refs):
        grad_ref, hint_ref, out_ref = refs[n:]
        out_ref[...] = sum_refs(refs[:n]) + grad_ref[...].astype(F32)

    return row_call(kernel, "input_update", [*terms, grad], [hint], [(F32, BLOCK)])[0]


def middle_back(terms, x, grads, grad_res, alpha):
    grad = sum_terms([*grads, grad_res])
    _, res, grad_mixed, share = step_back(x.astype(F32), sum_terms(terms), alpha, grad)
    return res.astype(BF), grad_mixed.astype(BF), share


def body(
    n_mp, x_bits, z_bits,
    hidden_in, doc_index, doc_position, w_query, w_key, w_value, w_out, w_up, w_gate, w_down,
    score_scale, up_scale, gate_scale, alpha_attention, alpha_feedforward, cotangent,
):
    depth, width = w_query.shape
    seq = doc_position.shape[0]
    me = lax.axis_index("mp").astype(jnp.int32).reshape(1)
    place = lax.axis_index("dp").astype(jnp.int32)
    x_first = x_bits + z_bits
    z_first = z_bits[:1] + x_bits + z_bits[1:]
    n_dp = 1 << len(x_first)

    tokens = jnp.arange(seq, dtype=jnp.int32)
    start = (tokens - doc_position).reshape(1, seq)
    steps = jnp.arange(HALF).astype(F32)
    inverse = jnp.exp(steps * (-2.0 * jnp.log(10000.0) / HEAD_DIM))
    angles = inverse[:, None] * doc_position.astype(F32)[None, :]
    cos, sin = jnp.cos(angles), jnp.sin(angles)
    scale = score_scale.reshape(width, 1)
    alpha_attention = alpha_attention.reshape(1, depth)
    alpha_feedforward = alpha_feedforward.reshape(1, depth)
    up_scale, gate_scale = up_scale.reshape(1, -1), gate_scale.reshape(1, -1)
    far_count = n_mp - 2

    def join(blocks):
        return jnp.concatenate(blocks, axis=0)

    def cut(parts):
        return [parts[b * BLOCK : (b + 1) * BLOCK] for b in range(parts.shape[0] // BLOCK)]

    near = slice(0, 2 * BLOCK)
    rest = slice(2 * BLOCK, None)
    pairs = range(width // PAIR)

    def columns(w, i):
        return w[:, i * PAIR : (i + 1) * PAIR]

    w_joint = jnp.concatenate(
        [columns(w, i) for i in pairs for w in (w_query, w_key, w_value)], axis=1
    )

    coming = gather_start(hidden_in, n_mp)
    x_near = [hidden_in, swap(hidden_in, 1, n_mp)]
    held = project(me, 0, x_near, [], w_query, w_key, w_value, cos, sin, scale)
    x_far = gather_finish(coming, held[0], n_mp)
    for i in range(0, far_count, 2):
        held = project(me, 2 + i, x_far[i : i + 2], held, w_query, w_key, w_value, cos, sin, scale)
    q, k, v, rq, rk = held
    o, l = attend(me, q, k, v, start)
    far_terms, sent = scatter_far(cut(dot_tn(o[:, rest], w_out).astype(BF)), n_mp)
    parts = cut(dot_tn(after(o, sent)[:, near], w_out).astype(BF))
    attn_terms = [parts[0], swap(parts[1], 1, n_mp), *far_terms]
    middle_low = middle_update(attn_terms, hidden_in, alpha_attention)

    def unit(rows):
        u = dot(rows, w_up)
        g = dot(rows, w_gate)
        gate = g * gate_scale
        inner = (u * up_scale * (gate / (1.0 + jnp.exp(-gate)))).astype(BF)
        return u.astype(BF), g.astype(BF), inner, dot(inner, w_down).astype(BF)

    coming = gather_start(middle_low, n_mp)
    mid_near = join([middle_low, swap(middle_low, 1, n_mp)])
    u0, g0, inner0, parts = unit(mid_near)
    mid_far = join(gather_finish(coming, parts, n_mp))
    u1, g1, inner1, far = unit(mid_far)
    far_terms, sent = scatter_far(cut(far), n_mp)
    parts = cut(after(parts, sent))
    x_all = jnp.concatenate([*x_near, *x_far[:-1], after(x_far[-1], sent)], axis=0)
    ff_terms = [parts[0], swap(parts[1], 1, n_mp), *far_terms]
    ff_terms[-1], x_all = lax.optimization_barrier((ff_terms[-1], x_all))
    layer_out, grad_res, grad_low, share_ff = last_update(ff_terms, middle_low, cotangent, alpha_feedforward)

    def unit_back(rows, u, g):
        grad = dot_nt(rows, w_down)
        u, g = u.astype(F32), g.astype(F32)
        gate = g * gate_scale
        sig = 1.0 / (1.0 + jnp.exp(-gate))
        by_up = grad * (gate * sig)
        by_gate = grad * (u * up_scale) * (sig * (1.0 + gate * (1.0 - sig)))
        du, dg = (by_up * up_scale).astype(BF), (by_gate * gate_scale).astype(BF)
        shares = jnp.stack([jnp.sum(by_up * u, axis=0), jnp.sum(by_gate * g, axis=0)])
        return du, dg, shares

    def unit_parts(du, dg):
        return (dot_nt(du, w_up) + dot_nt(dg, w_gate)).astype(BF)

    order = Order()
    coming = gather_start(grad_low, n_mp)
    g_near = [grad_low, order.fill(grad_low, swap(grad_low, 1, n_mp))]
    g_near = join(g_near)
    du0, dg0, shares0 = unit_back(g_near, u0, g0)
    near_parts = order.mark(unit_parts(du0, dg0))
    g_far = gather_finish(coming, near_parts, n_mp)
    g_far = join(g_far)
    grad_down = Reduction(order, [(dot_tn(g_near, inner0) + dot_tn(g_far, inner1)).astype(BF)], x_first, place)
    du1, dg1, shares1 = unit_back(order.tie(g_far), u1, g1)
    far = unit_parts(du1, dg1)
    far_terms, sent = scatter_far(cut(far), n_mp, order)
    order.mark(sent)
    unit_scales = shares0 + shares1

    def over_tokens(near, far):
        return (dot_tn(mid_near, near) + dot_tn(mid_far, order.tie(far))).astype(BF)

    grad_gate = Reduction(order, [over_tokens(dg0, dg1)], z_first, place)
    grad_up = Reduction(order, [over_tokens(du0, du1)], x_first, place)
    parts = cut(order.tie(near_parts))
    mid_terms = [parts[0], swap(parts[1], 1, n_mp), *far_terms]
    mid_terms[-1] = order.fill(sent, order.tie(mid_terms[-1]))
    grad_x, grad_low, share_attn = middle_back(attn_terms, hidden_in, mid_terms, grad_res, alpha_attention)
    order.mark(grad_low)

    coming = gather_start(grad_low, n_mp)
    a_near = [grad_low, swap(grad_low, 1, n_mp)]
    do_near = order.mark(dot_nt(w_out, order.tie(join(a_near))).astype(BF))
    grad_down.step()
    grad_gate.step()
    a_far = gather_finish(coming, order.last, n_mp, order, grad_low)
    do = order.mark(jnp.concatenate([do_near, dot_nt(w_out, join(a_far)).astype(BF)], axis=1))
    a_all = join(a_near + a_far)
    grad_up.step()

    def rows_first(grad):
        return with_layout_constraint(grad.astype(BF), Layout(major_to_minor=(0, 1)))

    grad_joint, grad_scale = attend_back(me, q, k, v, o, order.tie(do), l, start, rq, rk, cos, sin, scale)
    order.mark(grad_joint)
    grad_out = lax.dot_general(a_all, order.tie(o), (((0,), (1,)), ((), ())), preferred_element_type=F32)
    grad_out = rows_first(grad_out)
    shares = jnp.concatenate([share_attn, share_ff], axis=0).reshape(2 * n_mp, n_dp, -1)
    early = [shares.transpose(1, 0, 2), unit_scales.reshape(2, n_dp, -1).transpose(1, 0, 2)]
    joints = []
    for i in pairs:
        grads = rows_first(dot_tn(order.tie(x_all), grad_joint[:, 3 * i * PAIR : 3 * (i + 1) * PAIR]))
        grads = jnp.concatenate([grads, columns(grad_out, i)], axis=1)
        small = early if i == 0 else []
        if i == pairs[-1]:
            small = small + [grad_scale.reshape(1, n_dp, -1).transpose(1, 0, 2)]
        small = jnp.concatenate([t.reshape(n_dp, 1, -1) for t in small], axis=2).astype(BF)
        small = jnp.pad(small, ((0, 0), (0, 15), (0, 4 * PAIR - small.shape[2]))).reshape(-1, 4 * PAIR)
        joints.append(Reduction(order, [grads, small], x_first if i % 2 else z_first, place))
    while len(grad_up.bits) > 1:
        for reduction in (grad_up, grad_gate, grad_down):
            reduction.step()
    grad_up.merge([grad_gate, grad_down])
    far = dot_nt(order.tie(grad_joint)[rest], w_joint).astype(BF)
    far_terms, sent = scatter_far(cut(far), n_mp, order)
    order.mark(sent)
    joints[-1].step()
    parts = cut(dot_nt(order.tie(grad_joint)[near], w_joint).astype(BF))
    order.mark(parts[1])
    in_terms = [parts[0], swap(parts[1], 1, n_mp), *far_terms]
    for reduction in joints:
        while len(reduction.bits) > 1:
            reduction.step()
    in_terms[-1] = order.fill(sent, order.tie(in_terms[-1]))
    grad_input = input_update(in_terms, grad_x, order.hint)
    order.mark(grad_input)
    for reduction in joints:
        reduction.step()
    order.mark(grad_input)
    grad_up, grad_gate, grad_down = [h.astype(F32) + g.astype(F32) for h, g in grad_up.finish()]
    order.mark(grad_input)
    while joints[0].bits:
        for reduction in joints:
            reduction.step()
    ends = [order.tie(*reduction.held, reduction.got) for reduction in joints]
    small = [ends[0][1][0].astype(F32) + ends[0][2][depth // n_dp].astype(F32)]
    shares = small[0][: 2 * n_mp * (depth // n_mp // n_dp)].reshape(2, n_mp, -1)
    shares = [lax.dynamic_index_in_dim(shares, me[0] ^ b, 1, keepdims=False).astype(BF) for b in range(n_mp)]
    alpha = shares[0].astype(F32)
    pieces = {b: t for b, t in enumerate(shares) if b}
    bit = n_mp // 2
    while bit:
        for b in [b for b in list(pieces) if b & bit and b != bit]:
            pieces[b ^ bit] = add_low(pieces[b ^ bit], swap(pieces.pop(b), bit, n_mp))
        alpha = alpha + swap(pieces.pop(bit), bit, n_mp).astype(F32)
        bit //= 2
    scale_rows = small[0][shares[0].shape[1] * 2 * n_mp :]
    count = w_up.shape[1] // n_dp
    up_share, gate_share, score = scale_rows[:count], scale_rows[count : 2 * count], scale_rows[2 * count :]
    alpha_a, alpha_f = alpha[0], alpha[1]
    grad_query, grad_key, grad_value, grad_out, last = joint_sums(ends, width)
    score = (score if len(joints) == 1 else last[0])[: width // n_dp]
    grad_down = grad_down.T
    return (
        layer_out,
        grad_input,
        grad_query,
        grad_key,
        grad_value,
        grad_out,
        grad_up,
        grad_gate,
        grad_down,
        score,
        up_share,
        gate_share,
        alpha_a,
        alpha_f,
    )


def solution(mesh):
    n_dp, n_mp = mesh.shape["dp"], mesh.shape["mp"]
    bits = [1 << i for i in range(n_dp.bit_length() - 1)]
    cut = len(bits) // 2
    token = P(("dp", "mp"), None)
    split = P(("mp", "dp"))
    return jax.shard_map(
        partial(body, n_mp, bits[:cut], bits[cut:]),
        mesh=mesh,
        in_specs=(
            token, P("dp"), P("dp"), P(None, "mp"), P(None, "mp"), P(None, "mp"), P("mp", None),
            P(None, "mp"), P(None, "mp"), P("mp", None), P("mp"), P("mp"), P("mp"), P(), P(), token,
        ),
        out_specs=(
            token, token, P("dp", "mp"), P("dp", "mp"), P("dp", "mp"), P("mp", "dp"),
            P("dp", "mp"), P("dp", "mp"), P("mp", "dp"), split, split, split, split, split,
        ),
        check_vma=False,
    )
```
